32 devices in a mesh: gx: 8 (over z, y), gz: 4 (over x, core).
Axes of the slice: x: 2, y: 2, z: 4, core: 2. Of those that a mesh axis runs over, the one named last changes fastest.
Arguments:
- concentration: float32 [4, 32, 128, 512], P(None, 'gz', 'gx'), may hold values from -8 to 8
- facies: int32 [32, 128, 512], P('gz', 'gx'), may hold values from 0 to 5
- x_rates: float32 [6], replicated, may hold values from 2304 to 16384
- y_rates: float32 [6], replicated, may hold values from 4096 to 16384
- z_rates: float32 [6], replicated, may hold values from 0.05 to 0.45
- react_table: float32 [6, 4, 4], replicated, may hold values from -0.6 to 0.6
Outputs:
- updated: float32 [4, 32, 128, 512], P(None, 'gz', 'gx')
The draws below stay inside these ranges and needn't reach their ends.
All inputs are finite; a program needn't handle non-finite values.
Results may differ from the reference program's by a relative error of at most 0.0017.
Values sent between devices are 32-bit elements; how exact they have to be, the bound alone decides.
No kernel may reach another device: no remote copies, remote signals or barrier semaphores. Data moves between devices by JAX's collectives and lax.ppermute only.
A program may use at most 64 MiB of HBM per device.

```python
import math
import jax
import jax.numpy as jnp
from jax import lax

S = 4
NF = 6
NY = 512
PASSES = 2
NX = 128
NZ = 32


def draw_concentration(key, part):
    rough_part = jnp.clip(jax.random.normal(key, (S, NZ, NX, NY), jnp.float32), -6.0, 6.0)
    return rough_part


def with_ends(result, key, low, top_value):
    extent = result.shape
    index_at = [jax.random.randint(jax.random.fold_in(key, axis), (), 0, extent[axis]) for axis in range(len(extent))]
    result = result.at[tuple(index_at)].set(low)
    longest = extent.index(max(extent))
    index_at[longest] = (index_at[longest] + 1) % extent[longest]
    return result.at[tuple(index_at)].set(top_value)


def noise(rng, dims, spread, most, kind=jnp.bfloat16):
    return jnp.clip(spread * jax.random.normal(rng, dims, jnp.float32), -most, most).astype(kind)


def setup_inputs(seed: int = 0) -> dict:
    streams_of = jax.random.split(jax.random.key(seed), 7)
    return {
        "concentration": draw_concentration(jax.random.fold_in(streams_of[6], 71), 0),
        "facies": with_ends(jax.random.randint(streams_of[1], (NZ, NX, NY), 0, NF), jax.random.fold_in(streams_of[1], 1), 0, NF - 1).astype(jnp.int32),
        "x_rates": jnp.clip(jnp.exp(jax.random.uniform(streams_of[2], (NF,), jnp.float32, math.log(2304.0), math.log(16384.0))), 2304.0, 16384.0),
        "y_rates": jnp.clip(jnp.exp(jax.random.uniform(streams_of[3], (NF,), jnp.float32, math.log(4096.0), math.log(16384.0))), 4096.0, 16384.0),
        "z_rates": jnp.clip(jax.random.uniform(streams_of[4], (NF,), jnp.float32, 0.05, 0.45), 0.05, 0.45),
        "react_table": noise(streams_of[5], (NF, S, S), 0.15, 0.6, jnp.float32),
    }


def neighbour_faces(cells, direction):
    widths = [(1, 1) if dimension == direction else (0, 0) for dimension in range(cells.ndim)]
    padded = jnp.pad(cells, widths)
    length = padded.shape[direction]
    centre = lax.slice_in_dim(padded, 1, length - 1, axis=direction)
    before = lax.slice_in_dim(padded, 0, length - 2, axis=direction)
    beyond = lax.slice_in_dim(padded, 2, length, axis=direction)
    face_below = 2.0 * centre * before / (centre + before)
    face_above = 2.0 * centre * beyond / (centre + beyond)
    return face_below, face_above


def zero_padded(amounts, direction):
    widths = [(1, 1) if dimension == direction else (0, 0) for dimension in range(amounts.ndim)]
    return jnp.pad(amounts, widths)


def flux_terms(padded, amounts, face_below, face_above, direction):
    length = padded.shape[direction]
    before = lax.slice_in_dim(padded, 0, length - 2, axis=direction)
    beyond = lax.slice_in_dim(padded, 2, length, axis=direction)
    return face_above * (beyond - amounts) - face_below * (amounts - before)


def react_row(coefficients, amounts):
    total_term = coefficients[0] * amounts[0]
    for source in range(1, len(coefficients)):
        total_term = total_term + coefficients[source] * amounts[source]
    return total_term


def thomas_solve(face_below, face_above, source_values):
    def forward(carried, inputs_row):
        share_prev, value_prev = carried
        below_row, above_row, source_row = inputs_row
        excess_row = 1.0 + below_row * share_prev
        pivot_row = above_row + excess_row
        value_row = (source_row + below_row * value_prev) / pivot_row
        return (excess_row / pivot_row, value_row), (above_row / pivot_row, value_row)

    initial = (jnp.zeros(face_below.shape[1:], face_below.dtype), jnp.zeros(source_values.shape[1:], source_values.dtype))
    ignored, (ratios, values) = lax.scan(forward, initial, (face_below, face_above, source_values))

    def backward(solved_next, inputs_row):
        ratio_row, value_row = inputs_row
        solved_row = value_row + ratio_row * solved_next
        return solved_row, solved_row

    ignored_too, solved = lax.scan(backward, jnp.zeros(source_values.shape[1:], source_values.dtype), (ratios, values), reverse=True)
    return solved


def reference(concentration, facies, x_rates, y_rates, z_rates, react_table):
    below_x, above_x = neighbour_faces(x_rates[facies], 1)
    below_y, above_y = neighbour_faces(y_rates[facies], 2)
    below_z, above_z = neighbour_faces(z_rates[facies], 0)

    def plane_update(plane_inputs):
        plane_values, plane_below_x, plane_above_x, plane_below_y, plane_above_y = plane_inputs
        explicit_y = plane_values + flux_terms(zero_padded(plane_values, 2), plane_values, plane_below_y, plane_above_y, 2)
        x_solved = jnp.moveaxis(thomas_solve(plane_below_x, plane_above_x, jnp.moveaxis(explicit_y, 1, 0)), 0, 1)
        second = 2.0 * x_solved - explicit_y
        middle = thomas_solve(jnp.moveaxis(plane_below_y, 1, 0), jnp.moveaxis(plane_above_y, 1, 0), jnp.moveaxis(second, 2, 0))
        return jnp.moveaxis(middle, 0, 2)

    mapped = lax.map(plane_update, (jnp.moveaxis(concentration, 1, 0), below_x, above_x, below_y, above_y))
    amounts = jnp.moveaxis(mapped, 0, 1)
    for pass_index in range(PASSES):
        vertical_flux = flux_terms(zero_padded(amounts, 1), amounts, below_z[None], above_z[None], 1)
        reacted = jnp.stack([react_row([react_table[:, target, source][facies] for source in range(S)], amounts) for target in range(S)])
        amounts = amounts + vertical_flux + reacted
    return amounts
```

```python
import functools
import jax
import jax.numpy as jnp
from jax import lax
from jax.experimental import pallas as pl
from jax.experimental.pallas import tpu as pltpu
from jax.sharding import PartitionSpec as P

PASSES = 2
LANES = 128
SUBS = 8

VMEM = pl.BlockSpec(memory_space=pltpu.VMEM)
SMEM = pl.BlockSpec(memory_space=pltpu.SMEM)


def face(a, b):
    return 2.0 * a * b / (a + b)


def picked(table, masks):
    value = table(0)
    for index, mask in masks:
        value = jnp.where(mask, table(index), value)
    return value


def class_masks(facies, classes):
    return [(index, facies == index) for index in range(1, classes)]


def merge_blocks(left, right, joint):
    g1, lp, lq = left
    g2, lm, ln = right
    rq = 1.0 / (g1 + joint + lq)
    aq, bq = g1 * rq, joint * rq
    a = g1 * bq
    lp = lp + aq * lq
    lm = lm + bq * lq
    rm = 1.0 / (a + g2 + lm)
    am, bm = a * rm, g2 * rm
    return (a * bm, lp + am * lm, ln + bm * lm), (rq, aq, bq, rm, am, bm)


def merge_sources(fp, fq, fm, fn, factors):
    rq, aq, bq, rm, am, bm = factors
    fm = fm + bq * fq
    return fp + aq * fq + am * fm, fn + bm * fm, rq * fq, rm * fm


def split_values(first, last, hq, hm, factors):
    rq, aq, bq, rm, am, bm = factors
    um = hm + am * first + bm * last
    uq = hq + aq * first + bq * um
    return uq, um


def spread(ref, at, value):
    for lo in range(0, value.shape[1], LANES):
        ref[lo // LANES, at, :] = value[:, lo : lo + LANES]


def eliminate_x(dims, x_rates, y_rates, c_ref, fac_ref, ends_ref, rk_ref, ra_ref, h_ref, ky_ref, e_ref, rx_ref):
    species, nz, nx, ny, classes = dims
    rows = nz * nx
    lane = lax.broadcasted_iota(jnp.int32, (SUBS, ny), 1)
    not_last = lane < ny - 1
    for row in range(0, rows, SUBS):
        at = pl.ds(row, SUBS)
        masks = class_masks(fac_ref[at, :], classes)
        spread(rx_ref, at, picked(lambda i: x_rates[i], masks))
        ry = picked(lambda i: y_rates[i], masks)
        ky = jnp.where(not_last, face(ry, pltpu.roll(ry, ny - 1, 1)), 0.0)
        ky_ref[at, :] = ky
        for s in range(species):
            c = c_ref[s, at, :]
            flux = ky * (pltpu.roll(c, ny - 1, 1) - c)
            spread(e_ref.at[s], at, c + (flux - pltpu.roll(flux, 1, 1)))
    for lo in range(0, ny, LANES):
        lanes = pl.ds(lo, LANES)

        def rate_row(x):
            return rx_ref[lo // LANES, pl.ds(x, nz, stride=nx), :]

        def source_row(s, x):
            return e_ref[s, lo // LANES, pl.ds(x, nz, stride=nx), :]

        rate_first = rate_row(0)
        rate = rate_row(1)
        a = face(rate_first, rate)
        excess = jnp.ones_like(a)
        leak = jnp.ones_like(a)
        first = [source_row(s, 0) for s in range(species)]
        f = [source_row(s, 1) for s in range(species)]
        for x in range(1, nx - 1):
            rate_next = rate_row(x + 1)
            k = face(rate, rate_next)
            rate = rate_next
            r = 1.0 / (a + excess + k)
            rk, ra = k * r, a * r
            rk_ref[x, :, lanes] = rk
            ra_ref[x, :, lanes] = ra
            leak = leak + ra * excess
            a = a * rk
            excess = 1.0 + rk * excess
            for s in range(species):
                h_ref[s, x, :, lanes] = r * f[s]
                first[s] = first[s] + ra * f[s]
                f[s] = source_row(s, x + 1) + rk * f[s]
        for i, value in enumerate([a, leak, excess, rate_first, rate] + first + f):
            ends_ref[i, :, lanes] = value


def unpack_ends(values, species):
    return values[0:3], values[3], values[4], values[5 : 5 + species], values[5 + species :]


def merge_x(species, bit, is_last, next_bit, axis, own_ref, got_ref, *outs):
    side = (lax.axis_index(axis) >> bit) & 1 == 1
    next_side = (lax.axis_index(axis) >> next_bit) & 1 == 1
    ny = own_ref.shape[2]
    count = 5 + 2 * species
    for lo in range(0, ny, LANES):
        lanes = pl.ds(lo, LANES)
        own = [own_ref[i, :, lanes] for i in range(count)]
        got = [got_ref[i, :, lanes] for i in range(count)]
        left = [jnp.where(side, b, a) for a, b in zip(own, got)]
        right = [jnp.where(side, a, b) for a, b in zip(own, got)]
        lc, l_first, l_last, lfp, lfq = unpack_ends(left, species)
        rc, r_first, r_last, rfm, rfn = unpack_ends(right, species)
        (g, leak_p, leak_n), factors = merge_blocks(lc, rc, face(l_last, r_first))
        fp, fn, hq, hm = zip(*[merge_sources(*f4, factors) for f4 in zip(lfp, lfq, rfm, rfn)])
        saved = list(factors[1:3]) + list(factors[4:6]) + list(hq) + list(hm)
        for i, value in enumerate(saved):
            outs[1][i, :, lanes] = value
        if not is_last:
            for i, value in enumerate([g, leak_p, leak_n, l_first, r_last] + list(fp) + list(fn)):
                outs[0][i, :, lanes] = value
            continue
        emit_last(next_side, g, leak_p, leak_n, l_first, r_last, fp, fn, outs[0], outs[2], lanes)


def emit_last(next_side, g, leak_p, leak_n, rate_p, rate_n, fp, fn, message_ref, outer_ref, lanes):
    pick = lambda a, b: jnp.where(next_side, a, b)
    leak_out, leak_in = pick(leak_n, leak_p), pick(leak_p, leak_n)
    r = 1.0 / (g + leak_out)
    share = g * r
    message_ref[0, :, lanes] = leak_in + share * leak_out
    message_ref[1, :, lanes] = pick(rate_p, rate_n)
    outer_ref[0, :, lanes] = share
    for s in range(len(fp)):
        f_out, f_in = pick(fn[s], fp[s]), pick(fp[s], fn[s])
        message_ref[2 + s, :, lanes] = f_in + share * f_out
        outer_ref[1 + s, :, lanes] = r * f_out


def last_message(species, next_bit, axis, own_ref, message_ref, outer_ref):
    next_side = (lax.axis_index(axis) >> next_bit) & 1 == 1
    for lo in range(0, own_ref.shape[2], LANES):
        lanes = pl.ds(lo, LANES)
        coef, r_first, r_last, fp, fn = unpack_ends([own_ref[i, :, lanes] for i in range(5 + 2 * species)], species)
        emit_last(next_side, *coef, r_first, r_last, fp, fn, message_ref, outer_ref, lanes)


def y_levels(steps):
    sizes = []
    d = 1
    while d < SUBS:
        sizes.append(d)
        d *= 2
    return sizes


def exchange_sub(value, d, high):
    return jnp.where(high, pltpu.roll(value, d, 0), pltpu.roll(value, SUBS - d, 0))


def y_factors(dims, ky_ref, yr_ref, yk_ref, ya_ref, lv_ref, kt_ref):
    species, nz, nx, ny, classes = dims
    rows = nz * nx
    half = ny // SUBS // 2
    for lo in range(0, ny, LANES):
        kt_ref[pl.ds(lo, LANES), :] = ky_ref[:, pl.ds(lo, LANES)].T
    sub = lax.broadcasted_iota(jnp.int32, (SUBS, rows), 0)

    def k_row(i):
        return kt_ref[pl.ds(i, SUBS, stride=2 * half), :]

    blocks = []
    for group in range(2):
        a = k_row(group * half)
        excess = jnp.ones_like(a)
        leak = jnp.ones_like(a)
        for i in range(1, half - 1):
            k = k_row(group * half + i)
            r = 1.0 / (a + excess + k)
            rk, ra = k * r, a * r
            yr_ref[group, i] = r
            yk_ref[group, i] = rk
            ya_ref[group, i] = ra
            leak = leak + ra * excess
            a = a * rk
            excess = 1.0 + rk * excess
        blocks.append((a, leak, excess))
    block, factors = merge_blocks(blocks[0], blocks[1], k_row(half - 1))
    at = 0
    for value in factors:
        lv_ref[at] = value
        at += 1
    outer = k_row(2 * half - 1)
    levels = y_levels(half)
    for d in levels:
        high = sub & d != 0
        got = tuple(exchange_sub(v, d, high) for v in block)
        left = tuple(jnp.where(high, b, a) for a, b in zip(block, got))
        right = tuple(jnp.where(high, a, b) for a, b in zip(block, got))
        joint = outer
        base = sub & ~(2 * d - 1)
        joint = jnp.zeros_like(outer)
        for start in range(0, SUBS, 2 * d):
            edge = outer[start + d - 1 : start + d, :]
            joint = jnp.where(base == start, edge, joint)
        block, factors = merge_blocks(left, right, joint)
        for value in factors:
            lv_ref[at] = value
            at += 1
    g, leak_p, leak_n = block
    rn = 1.0 / (g + leak_n)
    rp = 1.0 / (leak_p + g * leak_n * rn)
    lv_ref[at] = rn
    lv_ref[at + 1] = g * rn
    lv_ref[at + 2] = rp


def z_tables(dims, z_rates, react, fac_ref, kz_ref, rz_ref, table_ref):
    species, nz, nx, ny, classes = dims
    rows = nz * nx
    for row in range(0, rows, SUBS):
        at = pl.ds(row, SUBS)
        masks = class_masks(fac_ref[at, :], classes)
        rz_ref[at, :] = picked(lambda i: z_rates[i], masks)
        for t in range(species):
            for s in range(species):
                table_ref[t * species + s, at, :] = picked(lambda i: react[i, t * species + s], masks)
    for row in range(0, rows - nx, SUBS):
        kz_ref[pl.ds(row, SUBS), :] = face(rz_ref[pl.ds(row, SUBS), :], rz_ref[pl.ds(row + nx, SUBS), :])


def reacted(table_ref, at, amounts, t):
    species = len(amounts)
    total = table_ref[t * species, at, :] * amounts[0]
    for s in range(1, species):
        total = total + table_ref[t * species + s, at, :] * amounts[s]
    return total


def solve_lines(dims, axes, bits, own_ref, got_ref, outer_ref, saved_refs, rk_ref, ra_ref, h_ref, c_ref,
                yr_ref, yk_ref, ya_ref, lv_ref, kz_ref, rz_ref, table_ref,
                m_ref, up_ref, down_ref, u_ref, vt_ref):
    species, nz, nx, ny, classes = dims
    rows = nz * nx
    half = ny // SUBS // 2
    index = lax.axis_index(axes[0])
    sides = [(index >> bit) & 1 == 1 for bit in bits]
    for lo in range(0, ny, LANES):
        lanes = pl.ds(lo, LANES)
        l1, r1 = own_ref[0, :, lanes], own_ref[1, :, lanes]
        l2, r2 = got_ref[0, :, lanes], got_ref[1, :, lanes]
        k = face(r1, r2)
        share = k / (l2 + k)
        inv = 1.0 / (l1 + share * l2)
        outer_share = outer_ref[0, :, lanes]
        level = [[saved[i, :, lanes] for i in range(4)] for saved in saved_refs]
        for s in range(species):
            inner = (own_ref[2 + s, :, lanes] + share * got_ref[2 + s, :, lanes]) * inv
            outer = outer_ref[1 + s, :, lanes] + outer_share * inner
            first = jnp.where(sides[-1], inner, outer)
            last = jnp.where(sides[-1], outer, inner)
            for n in reversed(range(len(saved_refs))):
                aq, bq, am, bm = level[n]
                hq = saved_refs[n][4 + s, :, lanes]
                hm = saved_refs[n][4 + species + s, :, lanes]
                um = hm + am * first + bm * last
                uq = hq + aq * first + bq * um
                first, last = jnp.where(sides[n], um, first), jnp.where(sides[n], last, uq)
            u_ref[s, lo // LANES, pl.ds(0, nz, stride=nx), :] = first
            u_ref[s, lo // LANES, pl.ds(nx - 1, nz, stride=nx), :] = last
            value = last
            for x in reversed(range(1, nx - 1)):
                value = h_ref[s, x, :, lanes] + ra_ref[x, :, lanes] * first + rk_ref[x, :, lanes] * value
                u_ref[s, lo // LANES, pl.ds(x, nz, stride=nx), :] = value
    for s in range(species):
        for lo in range(0, ny, LANES):
            lanes = pl.ds(lo, LANES)
            vt_ref[s, lanes, :] = (u_ref[s, lo // LANES] - c_ref[s, :, lanes]).T

    def at_step(group, i):
        return pl.ds(group * half + i, SUBS, stride=2 * half)

    sub = lax.broadcasted_iota(jnp.int32, (SUBS, rows), 0)
    ends = []
    for group in range(2):
        first = [vt_ref[s, at_step(group, 0), :] for s in range(species)]
        f = [vt_ref[s, at_step(group, 1), :] for s in range(species)]
        for i in range(1, half - 1):
            rk, ra = yk_ref[group, i], ya_ref[group, i]
            for s in range(species):
                first[s] = first[s] + ra * f[s]
                vt_ref[s, at_step(group, i), :] = f[s]
                f[s] = vt_ref[s, at_step(group, i + 1), :] + rk * f[s]
        ends.append((first, f))
    levels = y_levels(half)

    def factors_of(level):
        return [lv_ref[6 * level + i] for i in range(6)]

    solved = []
    for s in range(species):
        kept = []
        fac = factors_of(0)
        fp, fn, hq, hm = merge_sources(ends[0][0][s], ends[0][1][s], ends[1][0][s], ends[1][1][s], fac)
        kept.append((hq, hm))
        for number, d in enumerate(levels):
            high = sub & d != 0
            gp, gn = exchange_sub(fp, d, high), exchange_sub(fn, d, high)
            lp, lq = jnp.where(high, gp, fp), jnp.where(high, gn, fn)
            rm, rn = jnp.where(high, fp, gp), jnp.where(high, fn, gn)
            fp, fn, hq, hm = merge_sources(lp, lq, rm, rn, factors_of(number + 1))
            kept.append((hq, hm))
        top = 6 * (len(levels) + 1)
        rn, share, rp = lv_ref[top], lv_ref[top + 1], lv_ref[top + 2]
        first = (fp + share * fn) * rp
        last = rn * fn + share * first
        for number in reversed(range(len(levels))):
            high = sub & levels[number] != 0
            uq, um = split_values(first, last, *kept[number + 1], factors_of(number + 1))
            first, last = jnp.where(high, um, first), jnp.where(high, last, uq)
        uq, um = split_values(first, last, *kept[0], fac)
        solved.append(((first, uq), (um, last)))
    for group in range(2):
        value = [solved[s][group][1] for s in range(species)]
        for s in range(species):
            vt_ref[s, at_step(group, 0), :] = solved[s][group][0]
            vt_ref[s, at_step(group, half - 1), :] = value[s]
        for i in reversed(range(1, half - 1)):
            r, rk, ra = yr_ref[group, i], yk_ref[group, i], ya_ref[group, i]
            for s in range(species):
                value[s] = r * vt_ref[s, at_step(group, i), :] + ra * solved[s][group][0] + rk * value[s]
                vt_ref[s, at_step(group, i), :] = value[s]
    for s in range(species):
        for lo in range(0, ny, LANES):
            lanes = pl.ds(lo, LANES)
            m_ref[s, :, lanes] = c_ref[s, :, lanes] + 2.0 * vt_ref[s, lanes, :].T
    odd = lax.axis_index(axes[1]) & 1 == 1
    for part in range(0, nx, SUBS):
        here = pl.ds(part, SUBS)
        top, below_top = pl.ds(rows - nx + part, SUBS), pl.ds(rows - 2 * nx + part, SUBS)
        low, above_low = pl.ds(part, SUBS), pl.ds(nx + part, SUBS)
        m_top = [m_ref[s, top, :] for s in range(species)]
        m_low = [m_ref[s, low, :] for s in range(species)]
        k_top, k_low = kz_ref[below_top, :], kz_ref[low, :]
        for s in range(species):
            q_top = m_top[s] + reacted(table_ref, top, m_top, s) - k_top * (m_top[s] - m_ref[s, below_top, :])
            q_low = m_low[s] + reacted(table_ref, low, m_low, s) + k_low * (m_ref[s, above_low, :] - m_low[s])
            for n, (t, l) in enumerate(((m_top[s], m_low[s]), (q_top, q_low))):
                up_ref[n * species + s, here, :] = jnp.where(odd, l, t)
                down_ref[n * species + s, here, :] = jnp.where(odd, t, l)
        up_ref[2 * species, here, :] = jnp.where(odd, rz_ref[low, :], rz_ref[top, :])
        down_ref[2 * species, here, :] = jnp.where(odd, rz_ref[top, :], rz_ref[low, :])


def inner_passes(dims, m_ref, kz_ref, table_ref, p_ref, out_ref):
    species, nz, nx, ny, classes = dims

    def one_pass(source, target, first, last):
        for z in range(first, last):
            for part in range(0, nx, SUBS):
                row = z * nx + part
                at = pl.ds(row, SUBS)
                amounts = [source[s, at, :] for s in range(species)]
                for s in range(species):
                    total = amounts[s] + reacted(table_ref, at, amounts, s)
                    if z < nz - 1:
                        total = total + kz_ref[at, :] * (source[s, pl.ds(row + nx, SUBS), :] - amounts[s])
                    if z > 0:
                        total = total - kz_ref[pl.ds(row - nx, SUBS), :] * (amounts[s] - source[s, pl.ds(row - nx, SUBS), :])
                    target[s, at, :] = total

    one_pass(m_ref, p_ref, 0, nz)
    one_pass(p_ref, out_ref, 2, nz - 2)


def outer_passes(dims, axes, planes, m_ref, p_ref, inner_ref, a_ref, b_ref, kz_ref, rz_ref, table_ref, out_ref, n_ref):
    species, nz, nx, ny, classes = dims
    place = lax.axis_index(axes[1])
    odd = place & 1 == 1
    for row in range(2 * nx, (nz - 2) * nx, SUBS):
        for s in range(species):
            out_ref[s, pl.ds(row, SUBS), :] = inner_ref[s, pl.ds(row, SUBS), :]

    for part in range(0, nx, SUBS):
        here = pl.ds(part, SUBS)
        for top in (False, True):
            z, inward = (nz - 1, -1) if top else (0, 1)
            at = pl.ds(z * nx + part, SUBS)
            next_at = pl.ds((z + inward) * nx + part, SUBS)
            third_at = pl.ds((z + 2 * inward) * nx + part, SUBS)
            k_at = pl.ds((min(z, z + inward)) * nx + part, SUBS)
            k_next = pl.ds((min(z + inward, z + 2 * inward)) * nx + part, SUBS)
            exists = place < planes - 1 if top else place > 0

            def got(n):
                x, y = a_ref[n, here, :], b_ref[n, here, :]
                return jnp.where(odd, y, x) if top else jnp.where(odd, x, y)

            k = jnp.where(exists, face(rz_ref[at, :], got(2 * species)), 0.0)
            edge, beyond = [], []
            for s in range(species):
                flux = k * (got(s) - m_ref[s, at, :])
                edge.append(p_ref[s, at, :] + flux)
                beyond.append(got(species + s) - flux)
            ka, kb = kz_ref[k_at, :], kz_ref[k_next, :]
            second = [p_ref[s, next_at, :] for s in range(species)]
            for s in range(species):
                inside = ka * (second[s] - edge[s])
                out_ref[s, at, :] = edge[s] + reacted(table_ref, at, edge, s) + k * (beyond[s] - edge[s]) + inside
                out_ref[s, next_at, :] = (
                    second[s] + reacted(table_ref, next_at, second, s) - inside + kb * (p_ref[s, third_at, :] - second[s])
                )


def involution(size, step):
    return [(i, i ^ step) for i in range(size)]


def halo_pairs(gx, gz, start):
    pairs = []
    for j in range(gz):
        partner = j + 1 if (j - start) % 2 == 0 else j - 1
        for i in range(gx):
            if 0 <= partner < gz:
                pairs.append((i * gz + j, i * gz + partner))
            else:
                pairs.append((i * gz + j, (i ^ 1) * gz + j))
    return pairs


def shards(concentration, facies, x_rates, y_rates, z_rates, react_table, gx, gz):
    species, nz, nx, ny = concentration.shape
    classes = x_rates.shape[0]
    dims = (species, nz, nx, ny, classes)
    axes = ("gx", "gz")
    rows = nz * nx
    half = ny // SUBS // 2
    f32 = jnp.float32
    shape = lambda *d: jax.ShapeDtypeStruct(d, f32)
    params = pltpu.CompilerParams(vmem_limit_bytes=48 << 20)
    c = concentration.reshape(species, rows, ny)
    fac = facies.reshape(rows, ny)
    react = react_table.reshape(classes, species * species)
    rounds = gx.bit_length() - 1
    count = 5 + 2 * species

    ends, rk, ra, h, ky = pl.pallas_call(
        functools.partial(eliminate_x, dims),
        out_shape=[shape(count, nz, ny), shape(nx, nz, ny), shape(nx, nz, ny), shape(species, nx, nz, ny), shape(rows, ny)],
        in_specs=[SMEM, SMEM, VMEM, VMEM],
        out_specs=[VMEM] * 5,
        scratch_shapes=[pltpu.VMEM((species, ny // LANES, rows, LANES), f32), pltpu.VMEM((ny // LANES, rows, LANES), f32)],
        compiler_params=params,
        name="eliminate_x",
    )(x_rates, y_rates, c, fac)

    y_count = 6 * (1 + len(y_levels(half))) + 3
    y_fac = pl.pallas_call(
        functools.partial(y_factors, dims),
        out_shape=[shape(2, half, SUBS, rows)] * 3 + [shape(y_count, SUBS, rows)],
        in_specs=[VMEM],
        out_specs=[VMEM] * 4,
        scratch_shapes=[pltpu.VMEM((ny, rows), f32)],
        compiler_params=params,
        name="y_factors",
    )(ky)
    kz, rz, table = pl.pallas_call(
        functools.partial(z_tables, dims),
        out_shape=[shape(rows - nx, ny), shape(rows, ny), shape(species * species, rows, ny)],
        in_specs=[SMEM, SMEM, VMEM],
        out_specs=[VMEM] * 3,
        compiler_params=params,
        name="z_tables",
    )(z_rates, react, fac)

    saved = []
    own = ends
    if rounds == 1:
        own, outer = pl.pallas_call(
            functools.partial(last_message, species, 0, "gx"),
            out_shape=[shape(2 + species, nz, ny), shape(1 + species, nz, ny)],
            in_specs=[VMEM], out_specs=[VMEM] * 2, compiler_params=params, name="last_message",
        )(own)
    for bit in range(rounds - 1):
        got = lax.ppermute(own, "gx", involution(gx, 1 << bit))
        final = bit == rounds - 2
        message = shape(2 + species, nz, ny) if final else shape(count, nz, ny)
        out_shape = [message, shape(4 + 2 * species, nz, ny)] + ([shape(1 + species, nz, ny)] if final else [])
        merged = pl.pallas_call(
            functools.partial(merge_x, species, bit, final, bit + 1, "gx"),
            out_shape=out_shape,
            in_specs=[VMEM] * 2,
            out_specs=[VMEM] * len(out_shape),
            compiler_params=params,
            name=f"merge_x{bit}",
        )(own, got)
        own = merged[0]
        saved.append(merged[1])
        if final:
            outer = merged[2]
    got = lax.ppermute(own, "gx", involution(gx, 1 << (rounds - 1)))

    def solve(*refs):
        n = len(saved)
        solve_lines(dims, axes, list(range(rounds)), refs[0], refs[1], refs[2], refs[3 : 3 + n], *refs[3 + n :])

    operands = [own, got, outer] + saved + [rk, ra, h, c] + list(y_fac) + [kz, rz, table]
    m, to_a, to_b = pl.pallas_call(
        solve,
        out_shape=[shape(species, rows, ny), shape(2 * species + 1, nx, ny), shape(2 * species + 1, nx, ny)],
        in_specs=[VMEM] * len(operands),
        out_specs=[VMEM] * 3,
        scratch_shapes=[pltpu.VMEM((species, ny // LANES, rows, LANES), f32), pltpu.VMEM((species, ny, rows), f32)],
        compiler_params=params,
        name="solve_lines",
    )(*operands)

    got_a = lax.ppermute(to_a, axes, halo_pairs(gx, gz, 0))
    got_b = lax.ppermute(to_b, axes, halo_pairs(gx, gz, 1))
    p, inner = pl.pallas_call(
        functools.partial(inner_passes, dims),
        out_shape=[shape(species, rows, ny)] * 2,
        in_specs=[VMEM] * 3,
        out_specs=[VMEM] * 2,
        compiler_params=params,
        name="inner_passes",
    )(m, kz, table)
    out = pl.pallas_call(
        functools.partial(outer_passes, dims, axes, gz),
        out_shape=shape(species, rows, ny),
        in_specs=[VMEM] * 8,
        out_specs=VMEM,
        scratch_shapes=[pltpu.VMEM((SUBS, LANES), f32)],
        compiler_params=params,
        name="outer_passes",
    )(m, p, inner, got_a, got_b, kz, rz, table)
    return out.reshape(concentration.shape)


def solution(mesh):
    in_specs = (P(None, "gz", "gx", None), P("gz", "gx", None), P(), P(), P(), P())
    out_specs = P(None, "gz", "gx", None)
    body = functools.partial(shards, gx=mesh.shape["gx"], gz=mesh.shape["gz"])
    return jax.shard_map(body, mesh=mesh, in_specs=in_specs, out_specs=out_specs, check_vma=False)
```

```python
import functools
import jax
import jax.numpy as jnp
from jax import lax
from jax.experimental import pallas as pl
from jax.experimental.pallas import tpu as pltpu
from jax.sharding import PartitionSpec as P

PASSES = 2
LANES = 128
SUBS = 8

VMEM = pl.BlockSpec(memory_space=pltpu.VMEM)
ANY = pl.BlockSpec(memory_space=pl.ANY)
HBM = pl.BlockSpec(memory_space=pltpu.HBM)


def face(a, b):
    return 2.0 * a * b / (a + b)


def picked(table, masks):
    value = table(0)
    for index, mask in masks:
        value = jnp.where(mask, table(index), value)
    return value


def class_masks(facies, classes):
    return [(index, facies == index) for index in range(1, classes)]


def merge_blocks(left, right):
    g1, lp, lq = left
    g2, lm, ln = right
    leak = lq + lm
    r = 1.0 / (g1 + g2 + leak)
    before, after = g1 * r, g2 * r
    return (g1 * after, lp + before * leak, ln + after * leak), (r, before, after)


def spread(ref, at, value):
    for lo in range(0, value.shape[1], LANES):
        ref[lo // LANES, at, :] = value[:, lo : lo + LANES]


def eliminate_x(dims, xr_hbm, yr_hbm, c_hbm, fac_hbm, ends_ref, rk_ref, ra_ref, h_ref, ry_ref, c_ref, fac_ref,
                e_ref, rx_ref, ky_ref, x_rates, y_rates, sems):
    species, nz, nx, ny, classes = dims
    rows = nz * nx
    copies = [
        pltpu.make_async_copy(fac_hbm, fac_ref, sems.at[0]),
        pltpu.make_async_copy(xr_hbm, x_rates, sems.at[1]),
        pltpu.make_async_copy(yr_hbm, y_rates, sems.at[2]),
    ]
    arrivals = [pltpu.make_async_copy(c_hbm.at[s], c_ref.at[s], sems.at[3 + s]) for s in range(species)]
    for copy in copies + arrivals:
        copy.start()
    lane = lax.broadcasted_iota(jnp.int32, (SUBS, ny), 1)
    not_last = lane < ny - 1
    for copy in copies:
        copy.wait()
    for row in range(0, rows, SUBS):
        at = pl.ds(row, SUBS)
        masks = class_masks(fac_ref[at, :], classes)
        spread(rx_ref, at, picked(lambda i: x_rates[i], masks))
        ry = picked(lambda i: y_rates[i], masks)
        ry_ref[at, :] = ry
        ky_ref[at, :] = jnp.where(not_last, face(ry, pltpu.roll(ry, ny - 1, 1)), 0.0)
    for s in range(species):
        arrivals[s].wait()
        for row in range(0, rows, SUBS):
            at = pl.ds(row, SUBS)
            c = c_ref[s, at, :]
            flux = ky_ref[at, :] * (pltpu.roll(c, ny - 1, 1) - c)
            spread(e_ref.at[s], at, c + (flux - pltpu.roll(flux, 1, 1)))
    for lo in range(0, ny, LANES):
        lanes = pl.ds(lo, LANES)
        row_at = [pl.ds(x, nz, stride=nx) for x in range(nx)]
        rate = rx_ref[lo // LANES, row_at[0], :]
        a = 2.0 * rate
        excess = jnp.ones_like(a)
        leak = jnp.zeros_like(a)
        f = [e_ref[s, lo // LANES, row_at[0], :] for s in range(species)]
        first = [None] * species
        for x in range(nx):
            if x < nx - 1:
                rate_next = rx_ref[lo // LANES, row_at[x + 1], :]
                k = face(rate, rate_next)
                rate = rate_next
            else:
                k = 2.0 * rate
            r = 1.0 / (a + excess + k)
            rk, ra = k * r, a * r
            rk_ref[x, :, lanes] = rk
            ra_ref[x, :, lanes] = ra
            leak = leak + ra * excess
            a = a * rk
            excess = rk * excess
            if x < nx - 1:
                excess = 1.0 + excess
            for s in range(species):
                h_ref[s, x, :, lanes] = r * f[s]
                gain = ra * f[s]
                first[s] = gain if x == 0 else first[s] + gain
                f[s] = rk * f[s]
                if x < nx - 1:
                    f[s] = f[s] + e_ref[s, lo // LANES, row_at[x + 1], :]
        for i, value in enumerate([a, leak, excess] + first + f):
            ends_ref[i, :, lanes] = value


def side_of(axis, bit):
    return (lax.axis_index(axis) >> bit) & 1 == 1


def emit_block(final, next_side, block, fp, fn, lanes, out_ref, outer_ref):
    species = len(fp)
    if not final:
        for i, value in enumerate(list(block) + list(fp) + list(fn)):
            out_ref[i, :, lanes] = value
        return
    pick = lambda a, b: jnp.where(next_side, a, b)
    g, leak_p, leak_n = block
    leak_out, leak_in = pick(leak_n, leak_p), pick(leak_p, leak_n)
    r = 1.0 / (g + leak_out)
    share = g * r
    out_ref[0, :, lanes] = leak_in + share * leak_out
    outer_ref[0, :, lanes] = share
    for s in range(species):
        f_out, f_in = pick(fn[s], fp[s]), pick(fp[s], fn[s])
        out_ref[1 + s, :, lanes] = f_in + share * f_out
        outer_ref[1 + s, :, lanes] = r * f_out


def merge_x(species, bit, final, axis, own_ref, got_ref, after_ref, out_ref, saved_ref, outer_ref=None):
    side, next_side = side_of(axis, bit), side_of(axis, bit + 1)
    for lo in range(0, own_ref.shape[2], LANES):
        lanes = pl.ds(lo, LANES)
        own = [own_ref[i, :, lanes] for i in range(3 + 2 * species)]
        got = [got_ref[i, :, lanes] for i in range(3 + 2 * species)]
        left = [jnp.where(side, b, a) for a, b in zip(own, got)]
        right = [jnp.where(side, a, b) for a, b in zip(own, got)]
        block, (r, before, after) = merge_blocks(left[:3], right[:3])
        saved_ref[0, :, lanes] = before
        saved_ref[1, :, lanes] = after
        fp, fn = [], []
        for s in range(species):
            node = left[3 + species + s] + right[3 + s]
            fp.append(left[3 + s] + before * node)
            fn.append(right[3 + species + s] + after * node)
            saved_ref[2 + s, :, lanes] = r * node
        emit_block(final, next_side, block, fp, fn, lanes, out_ref, outer_ref)


def last_message(species, axis, own_ref, after_ref, out_ref, outer_ref):
    for lo in range(0, own_ref.shape[2], LANES):
        lanes = pl.ds(lo, LANES)
        own = [own_ref[i, :, lanes] for i in range(3 + 2 * species)]
        emit_block(True, side_of(axis, 0), own[:3], own[3 : 3 + species], own[3 + species :], lanes, out_ref, outer_ref)


def sub_levels():
    return [1 << n for n in range(SUBS.bit_length() - 1)]


def y_factors(dims, ry_ref, yr_ref, yk_ref, ya_ref, lv_ref, rt_ref):
    species, nz, nx, ny, classes = dims
    rows = nz * nx
    half = ny // SUBS // 2
    for lo in range(0, ny, LANES):
        rt_ref[pl.ds(lo, LANES), :] = ry_ref[:, pl.ds(lo, LANES)].T
    sub = lax.broadcasted_iota(jnp.int32, (SUBS, rows), 0)

    blocks = []
    for group in range(2):
        rates = [rt_ref[pl.ds(group * half + i, SUBS, stride=2 * half), :] for i in range(half)]
        a = 2.0 * rates[0]
        excess = jnp.ones_like(a)
        leak = jnp.zeros_like(a)
        for i in range(half):
            k = face(rates[i], rates[i + 1]) if i < half - 1 else 2.0 * rates[i]
            r = 1.0 / (a + excess + k)
            rk, ra = k * r, a * r
            yr_ref[group, i] = r
            yk_ref[group, i] = rk
            ya_ref[group, i] = ra
            leak = leak + ra * excess
            a = a * rk
            excess = rk * excess
            if i < half - 1:
                excess = 1.0 + excess
        blocks.append((a, leak, excess))
    block, factors = merge_blocks(*blocks)
    kept = list(factors)
    for d in sub_levels():
        high = sub & d != 0
        from_low = [pltpu.roll(v, d, 0) for v in block]
        from_high = [pltpu.roll(v, SUBS - d, 0) for v in block]
        left = [jnp.where(high, b, a) for a, b in zip(block, from_low)]
        right = [jnp.where(high, a, b) for a, b in zip(block, from_high)]
        block, factors = merge_blocks(left, right)
        kept += list(factors)
    g, leak_p, leak_n = block
    rn = 1.0 / (g + leak_n)
    kept += [rn, g * rn, 1.0 / (leak_p + g * leak_n * rn)]
    for i, value in enumerate(kept):
        lv_ref[i] = value


def z_tables(dims, z_hbm, react_hbm, fac_ref, after_ref, kz_ref, rz_ref, table_ref, z_rates, react, sems):
    species, nz, nx, ny, classes = dims
    rows = nz * nx
    copies = [pltpu.make_async_copy(z_hbm, z_rates, sems.at[0]), pltpu.make_async_copy(react_hbm, react, sems.at[1])]
    for copy in copies:
        copy.start()
    for copy in copies:
        copy.wait()
    for row in range(0, rows, SUBS):
        at = pl.ds(row, SUBS)
        masks = class_masks(fac_ref[at, :], classes)
        rz_ref[at, :] = picked(lambda i: z_rates[i], masks)
        for t in range(species):
            for s in range(species):
                table_ref[t * species + s, at, :] = picked(lambda i: react[t, s, i], masks)
    for row in range(0, rows - nx, SUBS):
        kz_ref[pl.ds(row, SUBS), :] = face(rz_ref[pl.ds(row, SUBS), :], rz_ref[pl.ds(row + nx, SUBS), :])


def reacted(table_ref, at, amounts, t):
    species = len(amounts)
    total = table_ref[t * species, at, :] * amounts[0]
    for s in range(1, species):
        total = total + table_ref[t * species + s, at, :] * amounts[s]
    return total


def solve_lines(dims, axes, bits, own_ref, got_ref, outer_ref, saved_refs, rk_ref, ra_ref, h_ref, c_ref,
                yr_ref, yk_ref, ya_ref, lv_ref, kz_ref, rz_ref, table_ref,
                m_ref, up_ref, down_ref, u_ref, vt_ref):
    species, nz, nx, ny, classes = dims
    rows = nz * nx
    half = ny // SUBS // 2
    index = lax.axis_index(axes[0])
    sides = [(index >> bit) & 1 == 1 for bit in bits]
    for lo in range(0, ny, LANES):
        lanes = pl.ds(lo, LANES)
        inv = 1.0 / (own_ref[0, :, lanes] + got_ref[0, :, lanes])
        outer_share = outer_ref[0, :, lanes]
        level = [(saved[0, :, lanes], saved[1, :, lanes]) for saved in saved_refs]
        for s in range(species):
            inner = (own_ref[1 + s, :, lanes] + got_ref[1 + s, :, lanes]) * inv
            outer = outer_ref[1 + s, :, lanes] + outer_share * inner
            first = jnp.where(sides[-1], inner, outer)
            last = jnp.where(sides[-1], outer, inner)
            for n in reversed(range(len(saved_refs))):
                before, after = level[n]
                node = saved_refs[n][2 + s, :, lanes] + before * first + after * last
                first, last = jnp.where(sides[n], node, first), jnp.where(sides[n], last, node)
            value = last
            for x in reversed(range(nx)):
                value = h_ref[s, x, :, lanes] + ra_ref[x, :, lanes] * first + rk_ref[x, :, lanes] * value
                u_ref[s, lo // LANES, pl.ds(x, nz, stride=nx), :] = value
    for s in range(species):
        for lo in range(0, ny, LANES):
            lanes = pl.ds(lo, LANES)
            vt_ref[s, lanes, :] = (u_ref[s, lo // LANES] - c_ref[s, :, lanes]).T

    def at_step(group, i):
        return pl.ds(group * half + i, SUBS, stride=2 * half)

    sub = lax.broadcasted_iota(jnp.int32, (SUBS, rows), 0)
    ends = []
    for group in range(2):
        f = [vt_ref[s, at_step(group, 0), :] for s in range(species)]
        first = [None] * species
        for i in range(half):
            rk, ra = yk_ref[group, i], ya_ref[group, i]
            for s in range(species):
                gain = ra * f[s]
                first[s] = gain if i == 0 else first[s] + gain
                if i > 0:
                    vt_ref[s, at_step(group, i), :] = f[s]
                f[s] = rk * f[s]
                if i < half - 1:
                    f[s] = f[s] + vt_ref[s, at_step(group, i + 1), :]
        ends.append((first, f))
    levels = sub_levels()
    highs = [sub & d != 0 for d in levels]
    factors = [[lv_ref[3 * n + i] for i in range(3)] for n in range(len(levels) + 2)]
    solved = []
    for s in range(species):
        r, before, after = factors[0]
        node = ends[0][1][s] + ends[1][0][s]
        fp, fn = ends[0][0][s] + before * node, ends[1][1][s] + after * node
        kept = [r * node]
        for n, d in enumerate(levels):
            r, before, after = factors[n + 1]
            node = jnp.where(highs[n], fp + pltpu.roll(fn, d, 0), fn + pltpu.roll(fp, SUBS - d, 0))
            fp, fn = (
                jnp.where(highs[n], pltpu.roll(fp, d, 0), fp) + before * node,
                jnp.where(highs[n], fn, pltpu.roll(fn, SUBS - d, 0)) + after * node,
            )
            kept.append(r * node)
        rn, share, rp = factors[-1]
        first = (fp + share * fn) * rp
        last = rn * fn + share * first
        for n in reversed(range(len(levels))):
            r, before, after = factors[n + 1]
            node = kept[n + 1] + before * first + after * last
            first, last = jnp.where(highs[n], node, first), jnp.where(highs[n], last, node)
        r, before, after = factors[0]
        node = kept[0] + before * first + after * last
        solved.append(((first, node), (node, last)))
    for group in range(2):
        value = [solved[s][group][1] for s in range(species)]
        for i in reversed(range(half)):
            r, rk, ra = yr_ref[group, i], yk_ref[group, i], ya_ref[group, i]
            for s in range(species):
                value[s] = r * vt_ref[s, at_step(group, i), :] + ra * solved[s][group][0] + rk * value[s]
                vt_ref[s, at_step(group, i), :] = value[s]
    for s in range(species):
        for lo in range(0, ny, LANES):
            lanes = pl.ds(lo, LANES)
            m_ref[s, :, lanes] = c_ref[s, :, lanes] + 2.0 * vt_ref[s, lanes, :].T
    odd = lax.axis_index(axes[1]) & 1 == 1
    for part in range(0, nx, SUBS):
        here = pl.ds(part, SUBS)
        top, below_top = pl.ds(rows - nx + part, SUBS), pl.ds(rows - 2 * nx + part, SUBS)
        low, above_low = pl.ds(part, SUBS), pl.ds(nx + part, SUBS)
        m_top = [m_ref[s, top, :] for s in range(species)]
        m_low = [m_ref[s, low, :] for s in range(species)]
        k_top, k_low = kz_ref[below_top, :], kz_ref[low, :]
        for s in range(species):
            q_top = m_top[s] + reacted(table_ref, top, m_top, s) - k_top * (m_top[s] - m_ref[s, below_top, :])
            q_low = m_low[s] + reacted(table_ref, low, m_low, s) + k_low * (m_ref[s, above_low, :] - m_low[s])
            for n, (t, l) in enumerate(((m_top[s], m_low[s]), (q_top, q_low))):
                up_ref[n * species + s, here, :] = jnp.where(odd, l, t)
                down_ref[n * species + s, here, :] = jnp.where(odd, t, l)
        up_ref[2 * species, here, :] = jnp.where(odd, rz_ref[low, :], rz_ref[top, :])
        down_ref[2 * species, here, :] = jnp.where(odd, rz_ref[top, :], rz_ref[low, :])


def inner_passes(dims, m_ref, kz_ref, table_ref, p_ref, out_hbm, out_ref, sems):
    species, nz, nx, ny, classes = dims

    def one_pass(source, target, z, s_done=None):
        for part in range(0, nx, SUBS):
            row = z * nx + part
            at = pl.ds(row, SUBS)
            amounts = [source[s, at, :] for s in range(species)]
            for s in range(species):
                total = amounts[s] + reacted(table_ref, at, amounts, s)
                if z < nz - 1:
                    total = total + kz_ref[at, :] * (source[s, pl.ds(row + nx, SUBS), :] - amounts[s])
                if z > 0:
                    total = total - kz_ref[pl.ds(row - nx, SUBS), :] * (amounts[s] - source[s, pl.ds(row - nx, SUBS), :])
                target[s, at, :] = total

    copies = []
    for z in range(nz):
        one_pass(m_ref, p_ref, z)
        if 3 <= z < nz - 1:
            one_pass(p_ref, out_ref, z - 1)
            planes = pl.ds((z - 1) * nx, nx)
            copies.append(pltpu.make_async_copy(out_ref.at[:, planes, :], out_hbm.at[:, planes, :], sems.at[len(copies)]))
            copies[-1].start()
    for copy in copies:
        copy.wait()


def outer_passes(dims, axes, planes, m_ref, p_ref, a_ref, b_ref, kz_ref, rz_ref, table_ref, inner_hbm, out_hbm, out_ref, sems):
    species, nz, nx, ny, classes = dims
    place = lax.axis_index(axes[1])
    odd = place & 1 == 1
    copies = []
    for top in (False, True):
        z, inward = (nz - 1, -1) if top else (0, 1)
        exists = place < planes - 1 if top else place > 0
        for part in range(0, nx, SUBS):
            here = pl.ds(part, SUBS)
            at = pl.ds(z * nx + part, SUBS)
            next_at = pl.ds((z + inward) * nx + part, SUBS)
            third_at = pl.ds((z + 2 * inward) * nx + part, SUBS)
            k_at = pl.ds((min(z, z + inward)) * nx + part, SUBS)
            k_next = pl.ds((min(z + inward, z + 2 * inward)) * nx + part, SUBS)

            def got(n):
                x, y = a_ref[n, here, :], b_ref[n, here, :]
                return jnp.where(odd, y, x) if top else jnp.where(odd, x, y)

            k = jnp.where(exists, face(rz_ref[at, :], got(2 * species)), 0.0)
            edge, beyond = [], []
            for s in range(species):
                flux = k * (got(s) - m_ref[s, at, :])
                edge.append(p_ref[s, at, :] + flux)
                beyond.append(got(species + s) - flux)
            ka, kb = kz_ref[k_at, :], kz_ref[k_next, :]
            second = [p_ref[s, next_at, :] for s in range(species)]
            mine, inner = pl.ds((2 if top else 0) * nx + part, SUBS), pl.ds((3 if top else 1) * nx + part, SUBS)
            for s in range(species):
                inside = ka * (second[s] - edge[s])
                out_ref[s, mine, :] = edge[s] + reacted(table_ref, at, edge, s) + k * (beyond[s] - edge[s]) + inside
                out_ref[s, inner, :] = (
                    second[s] + reacted(table_ref, next_at, second, s) - inside + kb * (p_ref[s, third_at, :] - second[s])
                )
        for n, plane in ((2, nz - 1), (3, nz - 2)) if top else ((0, 0), (1, 1)):
            copies.append(
                pltpu.make_async_copy(
                    out_ref.at[:, pl.ds(n * nx, nx), :], out_hbm.at[:, pl.ds(plane * nx, nx), :], sems.at[n]
                )
            )
            copies[-1].start()
    for copy in copies:
        copy.wait()


def involution(size, step):
    return [(i, i ^ step) for i in range(size)]


def halo_pairs(gx, gz, start):
    pairs = []
    for j in range(gz):
        partner = j + 1 if (j - start) % 2 == 0 else j - 1
        for i in range(gx):
            if 0 <= partner < gz:
                pairs.append((i * gz + j, i * gz + partner))
            else:
                pairs.append((i * gz + j, (i ^ 1) * gz + j))
    return pairs


def shards(concentration, facies, x_rates, y_rates, z_rates, react_table, gx, gz):
    species, nz, nx, ny = concentration.shape
    classes = x_rates.shape[0]
    dims = (species, nz, nx, ny, classes)
    axes = ("gx", "gz")
    rows = nz * nx
    half = ny // SUBS // 2
    f32 = jnp.float32
    shape = lambda *d: jax.ShapeDtypeStruct(d, f32)
    scratch = lambda *d: pltpu.VMEM(d, f32)
    dma = lambda n: pltpu.SemaphoreType.DMA((n,))

    def call(kernel, name, out_shape, in_specs, out_specs=None, scratch_shapes=(), **options):
        return pl.pallas_call(
            kernel,
            out_shape=out_shape,
            in_specs=in_specs,
            out_specs=out_specs or [VMEM] * len(out_shape),
            scratch_shapes=list(scratch_shapes),
            compiler_params=pltpu.CompilerParams(vmem_limit_bytes=8 << 20),
            name=name,
            **options,
        )

    in_hbm = lambda array: pltpu.with_memory_space_constraint(array, pltpu.HBM)
    react = jnp.transpose(react_table, (1, 2, 0))
    c = concentration.reshape(species, rows, ny)
    fac = facies.reshape(rows, ny)
    rounds = gx.bit_length() - 1
    assert gx == 1 << rounds and rounds > 0 and gz > 1 and nz >= 4
    count, few = 3 + 2 * species, 1 + species
    blocks = ny // LANES

    ends, rk, ra, h, ry, c, fac = call(
        functools.partial(eliminate_x, dims),
        "eliminate_x",
        [shape(count, nz, ny), shape(nx, nz, ny), shape(nx, nz, ny), shape(species, nx, nz, ny), shape(rows, ny),
         shape(species, rows, ny), jax.ShapeDtypeStruct((rows, ny), jnp.int32)],
        [HBM] * 4,
        scratch_shapes=[scratch(species, blocks, rows, LANES), scratch(blocks, rows, LANES), scratch(rows, ny),
                        pltpu.SMEM((classes,), f32), pltpu.SMEM((classes,), f32), dma(3 + species)],
    )(in_hbm(x_rates), in_hbm(y_rates), in_hbm(c), in_hbm(fac))

    y_fac = call(
        functools.partial(y_factors, dims),
        "y_factors",
        [shape(2, half, SUBS, rows)] * 3 + [shape(3 * (2 + len(sub_levels())), SUBS, rows)],
        [VMEM],
        scratch_shapes=[scratch(ny, rows)],
    )(ry)
    kz, rz, table = call(
        functools.partial(z_tables, dims),
        "z_tables",
        [shape(rows - nx, ny), shape(rows, ny), shape(species * species, rows, ny)],
        [HBM, HBM, VMEM, ANY],
        scratch_shapes=[pltpu.SMEM((classes,), f32), pltpu.SMEM(react.shape, f32), dma(2)],
    )(in_hbm(z_rates), in_hbm(react), fac, ends)

    saved, own = [], ends
    side_work = [y_fac[3], table]
    for bit in range(rounds - 1):
        got = lax.ppermute(own, "gx", involution(gx, 1 << bit))
        final = bit == rounds - 2
        out_shape = [shape(few if final else count, nz, ny), shape(2 + species, nz, ny)] + [shape(few, nz, ny)] * final
        merged = call(
            functools.partial(merge_x, species, bit, final, "gx"), f"merge_x{bit}", out_shape, [VMEM, VMEM, ANY]
        )(own, got, side_work[min(bit, 1)])
        own = merged[0]
        saved.append(merged[1])
    if rounds > 1:
        outer = merged[2]
    else:
        own, outer = call(
            functools.partial(last_message, species, "gx"), "last_message", [shape(few, nz, ny)] * 2, [VMEM, ANY]
        )(own, table)
    got = lax.ppermute(own, "gx", involution(gx, 1 << (rounds - 1)))

    def solve(*refs):
        n = len(saved)
        solve_lines(dims, axes, list(range(rounds)), refs[0], refs[1], refs[2], refs[3 : 3 + n], *refs[3 + n :])

    operands = [own, got, outer] + saved + [rk, ra, h, c] + list(y_fac) + [kz, rz, table]
    m, to_a, to_b = call(
        solve,
        "solve_lines",
        [shape(species, rows, ny), shape(2 * species + 1, nx, ny), shape(2 * species + 1, nx, ny)],
        [VMEM] * len(operands),
        scratch_shapes=[scratch(species, blocks, rows, LANES), scratch(species, ny, rows)],
    )(*operands)

    got_a = lax.ppermute(to_a, axes, halo_pairs(gx, gz, 0))
    got_b = lax.ppermute(to_b, axes, halo_pairs(gx, gz, 1))
    p, inner = call(
        functools.partial(inner_passes, dims),
        "inner_passes",
        [shape(species, rows, ny)] * 2,
        [VMEM] * 3,
        [VMEM, HBM],
        scratch_shapes=[scratch(species, rows, ny), dma(nz - 4)],
    )(m, kz, table)
    (out,) = call(
        functools.partial(outer_passes, dims, axes, gz),
        "outer_passes",
        [shape(species, rows, ny)],
        [VMEM] * 7 + [HBM],
        [HBM],
        scratch_shapes=[scratch(species, 4 * nx, ny), dma(4)],
        input_output_aliases={7: 0},
    )(m, p, got_a, got_b, kz, rz, table, inner)
    return out.reshape(concentration.shape)


def solution(mesh):
    in_specs = (P(None, "gz", "gx", None), P("gz", "gx", None), P(), P(), P(), P())
    out_specs = P(None, "gz", "gx", None)
    body = functools.partial(shards, gx=mesh.shape["gx"], gz=mesh.shape["gz"])
    return jax.shard_map(body, mesh=mesh, in_specs=in_specs, out_specs=out_specs, check_vma=False)
```

```python
import functools
import jax
import jax.numpy as jnp
from jax import lax
from jax.experimental import pallas as pl
from jax.experimental.pallas import tpu as pltpu
from jax.sharding import PartitionSpec as P

PASSES = 2
LANES = 128
SUBS = 8

VMEM = pl.BlockSpec(memory_space=pltpu.VMEM)
ANY = pl.BlockSpec(memory_space=pl.ANY)
HBM = pl.BlockSpec(memory_space=pltpu.HBM)


def face(a, b):
    return 2.0 * a * b / (a + b)


def picked(table, masks):
    value = table(0)
    for index, mask in masks:
        value = jnp.where(mask, table(index), value)
    return value


def class_masks(facies, classes):
    return [(index, facies == index) for index in range(1, classes)]


def merge_blocks(left, right):
    g1, lp, lq = left
    g2, lm, ln = right
    leak = lq + lm
    r = 1.0 / (g1 + g2 + leak)
    before, after = g1 * r, g2 * r
    return (g1 * after, lp + before * leak, ln + after * leak), (r, before, after)


def apart(row, length):
    return pl.ds(row + row // length, SUBS)


def spread(ref, at, value):
    for lo in range(0, value.shape[1], LANES):
        ref[lo // LANES, at, :] = value[:, lo : lo + LANES]


def eliminate_x(dims, xr_hbm, yr_hbm, c_hbm, fac_hbm, ends_ref, rk_ref, ra_ref, h_ref, ry_ref, c_ref, fac_ref,
                e_ref, rx_ref, ky_ref, x_rates, y_rates, sems):
    species, nz, nx, ny, classes = dims
    rows = nz * nx
    copies = [
        pltpu.make_async_copy(fac_hbm, fac_ref, sems.at[0]),
        pltpu.make_async_copy(xr_hbm, x_rates, sems.at[1]),
        pltpu.make_async_copy(yr_hbm, y_rates, sems.at[2]),
    ]
    arrivals = [pltpu.make_async_copy(c_hbm.at[s], c_ref.at[s], sems.at[3 + s]) for s in range(species)]
    for copy in copies + arrivals:
        copy.start()
    lane = lax.broadcasted_iota(jnp.int32, (SUBS, ny), 1)
    not_last = lane < ny - 1
    for copy in copies:
        copy.wait()
    for row in range(0, rows, SUBS):
        at = pl.ds(row, SUBS)
        masks = class_masks(fac_ref[at, :], classes)
        spread(rx_ref, apart(row, nx), picked(lambda i: x_rates[i], masks))
        ry = picked(lambda i: y_rates[i], masks)
        ry_ref[at, :] = ry
        ky_ref[at, :] = jnp.where(not_last, face(ry, pltpu.roll(ry, ny - 1, 1)), 0.0)
    for s in range(species):
        arrivals[s].wait()
        for row in range(0, rows, SUBS):
            at = pl.ds(row, SUBS)
            c = c_ref[s, at, :]
            flux = ky_ref[at, :] * (pltpu.roll(c, ny - 1, 1) - c)
            spread(e_ref.at[s], apart(row, nx), c + (flux - pltpu.roll(flux, 1, 1)))
    for lo in range(0, ny, LANES):
        lanes = pl.ds(lo, LANES)
        row_at = [pl.ds(x, nz, stride=nx + 1) for x in range(nx)]
        rate = rx_ref[lo // LANES, row_at[0], :]
        a = 2.0 * rate
        excess = jnp.ones_like(a)
        leak = jnp.zeros_like(a)
        f = [e_ref[s, lo // LANES, row_at[0], :] for s in range(species)]
        first = [None] * species
        for x in range(nx):
            if x < nx - 1:
                rate_next = rx_ref[lo // LANES, row_at[x + 1], :]
                k = face(rate, rate_next)
                rate = rate_next
            else:
                k = 2.0 * rate
            r = 1.0 / (a + excess + k)
            rk, ra = k * r, a * r
            rk_ref[x, :, lanes] = rk
            ra_ref[x, :, lanes] = ra
            leak = leak + ra * excess
            a = a * rk
            excess = rk * excess
            if x < nx - 1:
                excess = 1.0 + excess
            for s in range(species):
                h_ref[s, x, :, lanes] = r * f[s]
                gain = ra * f[s]
                first[s] = gain if x == 0 else first[s] + gain
                f[s] = rk * f[s]
                if x < nx - 1:
                    f[s] = f[s] + e_ref[s, lo // LANES, row_at[x + 1], :]
        for i, value in enumerate([a, leak, excess] + first + f):
            ends_ref[i, :, lanes] = value


def side_of(axis, bit):
    return (lax.axis_index(axis) >> bit) & 1 == 1


def emit_block(final, next_side, block, fp, fn, lanes, out_ref, outer_ref):
    species = len(fp)
    if not final:
        for i, value in enumerate(list(block) + list(fp) + list(fn)):
            out_ref[i, :, lanes] = value
        return
    pick = lambda a, b: jnp.where(next_side, a, b)
    g, leak_p, leak_n = block
    leak_out, leak_in = pick(leak_n, leak_p), pick(leak_p, leak_n)
    r = 1.0 / (g + leak_out)
    share = g * r
    out_ref[0, :, lanes] = leak_in + share * leak_out
    outer_ref[0, :, lanes] = share
    for s in range(species):
        f_out, f_in = pick(fn[s], fp[s]), pick(fp[s], fn[s])
        out_ref[1 + s, :, lanes] = f_in + share * f_out
        outer_ref[1 + s, :, lanes] = r * f_out


def merge_x(species, bit, final, axis, own_ref, got_ref, after_ref, out_ref, saved_ref, outer_ref=None):
    side, next_side = side_of(axis, bit), side_of(axis, bit + 1)
    for lo in range(0, own_ref.shape[2], LANES):
        lanes = pl.ds(lo, LANES)
        own = [own_ref[i, :, lanes] for i in range(3 + 2 * species)]
        got = [got_ref[i, :, lanes] for i in range(3 + 2 * species)]
        left = [jnp.where(side, b, a) for a, b in zip(own, got)]
        right = [jnp.where(side, a, b) for a, b in zip(own, got)]
        block, (r, before, after) = merge_blocks(left[:3], right[:3])
        saved_ref[0, :, lanes] = before
        saved_ref[1, :, lanes] = after
        fp, fn = [], []
        for s in range(species):
            node = left[3 + species + s] + right[3 + s]
            fp.append(left[3 + s] + before * node)
            fn.append(right[3 + species + s] + after * node)
            saved_ref[2 + s, :, lanes] = r * node
        emit_block(final, next_side, block, fp, fn, lanes, out_ref, outer_ref)


def last_message(species, axis, own_ref, after_ref, out_ref, outer_ref):
    for lo in range(0, own_ref.shape[2], LANES):
        lanes = pl.ds(lo, LANES)
        own = [own_ref[i, :, lanes] for i in range(3 + 2 * species)]
        emit_block(True, side_of(axis, 0), own[:3], own[3 : 3 + species], own[3 + species :], lanes, out_ref, outer_ref)


def sub_levels():
    return [1 << n for n in range(SUBS.bit_length() - 1)]


def y_factors(dims, ry_ref, yr_ref, yk_ref, ya_ref, lv_ref, rt_ref):
    species, nz, nx, ny, classes = dims
    rows = nz * nx
    half = ny // SUBS // 2
    for lo in range(0, ny, LANES):
        turned = ry_ref[:, pl.ds(lo, LANES)].T
        for y in range(0, LANES, SUBS):
            rt_ref[apart(lo + y, 2 * half), :] = turned[y : y + SUBS]
    sub = lax.broadcasted_iota(jnp.int32, (SUBS, rows), 0)

    blocks = []
    for group in range(2):
        rates = [rt_ref[pl.ds(group * half + i, SUBS, stride=2 * half + 1), :] for i in range(half)]
        a = 2.0 * rates[0]
        excess = jnp.ones_like(a)
        leak = jnp.zeros_like(a)
        for i in range(half):
            k = face(rates[i], rates[i + 1]) if i < half - 1 else 2.0 * rates[i]
            r = 1.0 / (a + excess + k)
            rk, ra = k * r, a * r
            yr_ref[group, i] = r
            yk_ref[group, i] = rk
            ya_ref[group, i] = ra
            leak = leak + ra * excess
            a = a * rk
            excess = rk * excess
            if i < half - 1:
                excess = 1.0 + excess
        blocks.append((a, leak, excess))
    block, factors = merge_blocks(*blocks)
    kept = list(factors)
    for d in sub_levels():
        high = sub & d != 0
        from_low = [pltpu.roll(v, d, 0) for v in block]
        from_high = [pltpu.roll(v, SUBS - d, 0) for v in block]
        left = [jnp.where(high, b, a) for a, b in zip(block, from_low)]
        right = [jnp.where(high, a, b) for a, b in zip(block, from_high)]
        block, factors = merge_blocks(left, right)
        kept += list(factors)
    g, leak_p, leak_n = block
    rn = 1.0 / (g + leak_n)
    kept += [rn, g * rn, 1.0 / (leak_p + g * leak_n * rn)]
    for i, value in enumerate(kept):
        lv_ref[i] = value


def z_tables(dims, z_hbm, react_hbm, fac_ref, after_ref, kz_ref, rz_ref, table_ref, z_rates, react, sems):
    species, nz, nx, ny, classes = dims
    rows = nz * nx
    copies = [pltpu.make_async_copy(z_hbm, z_rates, sems.at[0]), pltpu.make_async_copy(react_hbm, react, sems.at[1])]
    for copy in copies:
        copy.start()
    for copy in copies:
        copy.wait()
    for row in range(0, rows, SUBS):
        at = pl.ds(row, SUBS)
        masks = class_masks(fac_ref[at, :], classes)
        rz_ref[at, :] = picked(lambda i: z_rates[i], masks)
        for t in range(species):
            for s in range(species):
                table_ref[t * species + s, at, :] = picked(lambda i: react[t, s, i], masks)
    for row in range(0, rows - nx, SUBS):
        kz_ref[pl.ds(row, SUBS), :] = face(rz_ref[pl.ds(row, SUBS), :], rz_ref[pl.ds(row + nx, SUBS), :])


def reacted(table_ref, at, amounts, t):
    species = len(amounts)
    total = table_ref[t * species, at, :] * amounts[0]
    for s in range(1, species):
        total = total + table_ref[t * species + s, at, :] * amounts[s]
    return total


def solve_lines(dims, axes, bits, own_ref, got_ref, outer_ref, saved_refs, rk_ref, ra_ref, h_ref, c_ref,
                yr_ref, yk_ref, ya_ref, lv_ref, kz_ref, rz_ref, table_ref,
                m_ref, up_ref, down_ref, u_ref, vt_ref):
    species, nz, nx, ny, classes = dims
    rows = nz * nx
    half = ny // SUBS // 2
    index = lax.axis_index(axes[0])
    sides = [(index >> bit) & 1 == 1 for bit in bits]
    for lo in range(0, ny, LANES):
        lanes = pl.ds(lo, LANES)
        inv = 1.0 / (own_ref[0, :, lanes] + got_ref[0, :, lanes])
        outer_share = outer_ref[0, :, lanes]
        level = [(saved[0, :, lanes], saved[1, :, lanes]) for saved in saved_refs]
        for s in range(species):
            inner = (own_ref[1 + s, :, lanes] + got_ref[1 + s, :, lanes]) * inv
            outer = outer_ref[1 + s, :, lanes] + outer_share * inner
            first = jnp.where(sides[-1], inner, outer)
            last = jnp.where(sides[-1], outer, inner)
            for n in reversed(range(len(saved_refs))):
                before, after = level[n]
                node = saved_refs[n][2 + s, :, lanes] + before * first + after * last
                first, last = jnp.where(sides[n], node, first), jnp.where(sides[n], last, node)
            value = last
            for x in reversed(range(nx)):
                value = h_ref[s, x, :, lanes] + ra_ref[x, :, lanes] * first + rk_ref[x, :, lanes] * value
                u_ref[s, lo // LANES, pl.ds(x, nz, stride=nx + 1), :] = value
    for s in range(species):
        for lo in range(0, ny, LANES):
            lanes = pl.ds(lo, LANES)
            pieces = [
                u_ref[s, lo // LANES, apart(row, nx), :] - c_ref[s, pl.ds(row, SUBS), lanes]
                for row in range(0, rows, SUBS)
            ]
            turned = jnp.concatenate(pieces, axis=0).T
            for y in range(0, LANES, SUBS):
                vt_ref[s, apart(lo + y, 2 * half), :] = turned[y : y + SUBS]

    def at_step(group, i):
        return pl.ds(group * half + i, SUBS, stride=2 * half + 1)

    sub = lax.broadcasted_iota(jnp.int32, (SUBS, rows), 0)
    ends = []
    for group in range(2):
        f = [vt_ref[s, at_step(group, 0), :] for s in range(species)]
        first = [None] * species
        for i in range(half):
            rk, ra = yk_ref[group, i], ya_ref[group, i]
            for s in range(species):
                gain = ra * f[s]
                first[s] = gain if i == 0 else first[s] + gain
                if i > 0:
                    vt_ref[s, at_step(group, i), :] = f[s]
                f[s] = rk * f[s]
                if i < half - 1:
                    f[s] = f[s] + vt_ref[s, at_step(group, i + 1), :]
        ends.append((first, f))
    levels = sub_levels()
    highs = [sub & d != 0 for d in levels]
    factors = [[lv_ref[3 * n + i] for i in range(3)] for n in range(len(levels) + 2)]
    solved = []
    for s in range(species):
        r, before, after = factors[0]
        node = ends[0][1][s] + ends[1][0][s]
        fp, fn = ends[0][0][s] + before * node, ends[1][1][s] + after * node
        kept = [r * node]
        for n, d in enumerate(levels):
            r, before, after = factors[n + 1]
            node = jnp.where(highs[n], fp + pltpu.roll(fn, d, 0), fn + pltpu.roll(fp, SUBS - d, 0))
            fp, fn = (
                jnp.where(highs[n], pltpu.roll(fp, d, 0), fp) + before * node,
                jnp.where(highs[n], fn, pltpu.roll(fn, SUBS - d, 0)) + after * node,
            )
            kept.append(r * node)
        rn, share, rp = factors[-1]
        first = (fp + share * fn) * rp
        last = rn * fn + share * first
        for n in reversed(range(len(levels))):
            r, before, after = factors[n + 1]
            node = kept[n + 1] + before * first + after * last
            first, last = jnp.where(highs[n], node, first), jnp.where(highs[n], last, node)
        r, before, after = factors[0]
        node = kept[0] + before * first + after * last
        solved.append(((first, node), (node, last)))
    for group in range(2):
        value = [solved[s][group][1] for s in range(species)]
        for i in reversed(range(half)):
            r, rk, ra = yr_ref[group, i], yk_ref[group, i], ya_ref[group, i]
            for s in range(species):
                value[s] = r * vt_ref[s, at_step(group, i), :] + ra * solved[s][group][0] + rk * value[s]
                vt_ref[s, at_step(group, i), :] = value[s]
    for s in range(species):
        for lo in range(0, ny, LANES):
            lanes = pl.ds(lo, LANES)
            pieces = [vt_ref[s, apart(lo + y, 2 * half), :] for y in range(0, LANES, SUBS)]
            m_ref[s, :, lanes] = c_ref[s, :, lanes] + 2.0 * jnp.concatenate(pieces, axis=0).T
    odd = lax.axis_index(axes[1]) & 1 == 1
    for part in range(0, nx, SUBS):
        here = pl.ds(part, SUBS)
        top, below_top = pl.ds(rows - nx + part, SUBS), pl.ds(rows - 2 * nx + part, SUBS)
        low, above_low = pl.ds(part, SUBS), pl.ds(nx + part, SUBS)
        m_top = [m_ref[s, top, :] for s in range(species)]
        m_low = [m_ref[s, low, :] for s in range(species)]
        k_top, k_low = kz_ref[below_top, :], kz_ref[low, :]
        for s in range(species):
            q_top = m_top[s] + reacted(table_ref, top, m_top, s) - k_top * (m_top[s] - m_ref[s, below_top, :])
            q_low = m_low[s] + reacted(table_ref, low, m_low, s) + k_low * (m_ref[s, above_low, :] - m_low[s])
            for n, (t, l) in enumerate(((m_top[s], m_low[s]), (q_top, q_low))):
                up_ref[n * species + s, here, :] = jnp.where(odd, l, t)
                down_ref[n * species + s, here, :] = jnp.where(odd, t, l)
        up_ref[2 * species, here, :] = jnp.where(odd, rz_ref[low, :], rz_ref[top, :])
        down_ref[2 * species, here, :] = jnp.where(odd, rz_ref[top, :], rz_ref[low, :])


def inner_passes(dims, m_ref, kz_ref, table_ref, p_ref, out_hbm, out_ref, sems):
    species, nz, nx, ny, classes = dims

    def one_pass(source, target, z, s_done=None):
        for part in range(0, nx, SUBS):
            row = z * nx + part
            at = pl.ds(row, SUBS)
            amounts = [source[s, at, :] for s in range(species)]
            for s in range(species):
                total = amounts[s] + reacted(table_ref, at, amounts, s)
                if z < nz - 1:
                    total = total + kz_ref[at, :] * (source[s, pl.ds(row + nx, SUBS), :] - amounts[s])
                if z > 0:
                    total = total - kz_ref[pl.ds(row - nx, SUBS), :] * (amounts[s] - source[s, pl.ds(row - nx, SUBS), :])
                target[s, at, :] = total

    copies = []
    for z in range(nz):
        one_pass(m_ref, p_ref, z)
        if 3 <= z < nz - 1:
            one_pass(p_ref, out_ref, z - 1)
            planes = pl.ds((z - 1) * nx, nx)
            copies.append(pltpu.make_async_copy(out_ref.at[:, planes, :], out_hbm.at[:, planes, :], sems.at[len(copies)]))
            copies[-1].start()
    for copy in copies:
        copy.wait()


def outer_passes(dims, axes, planes, m_ref, p_ref, a_ref, b_ref, kz_ref, rz_ref, table_ref, inner_hbm, out_hbm, out_ref, sems):
    species, nz, nx, ny, classes = dims
    place = lax.axis_index(axes[1])
    odd = place & 1 == 1
    copies = []
    for top in (False, True):
        z, inward = (nz - 1, -1) if top else (0, 1)
        exists = place < planes - 1 if top else place > 0
        for part in range(0, nx, SUBS):
            here = pl.ds(part, SUBS)
            at = pl.ds(z * nx + part, SUBS)
            next_at = pl.ds((z + inward) * nx + part, SUBS)
            third_at = pl.ds((z + 2 * inward) * nx + part, SUBS)
            k_at = pl.ds((min(z, z + inward)) * nx + part, SUBS)
            k_next = pl.ds((min(z + inward, z + 2 * inward)) * nx + part, SUBS)

            def got(n):
                x, y = a_ref[n, here, :], b_ref[n, here, :]
                return jnp.where(odd, y, x) if top else jnp.where(odd, x, y)

            k = jnp.where(exists, face(rz_ref[at, :], got(2 * species)), 0.0)
            edge, beyond = [], []
            for s in range(species):
                flux = k * (got(s) - m_ref[s, at, :])
                edge.append(p_ref[s, at, :] + flux)
                beyond.append(got(species + s) - flux)
            ka, kb = kz_ref[k_at, :], kz_ref[k_next, :]
            second = [p_ref[s, next_at, :] for s in range(species)]
            mine, inner = pl.ds((2 if top else 0) * nx + part, SUBS), pl.ds((3 if top else 1) * nx + part, SUBS)
            for s in range(species):
                inside = ka * (second[s] - edge[s])
                out_ref[s, mine, :] = edge[s] + reacted(table_ref, at, edge, s) + k * (beyond[s] - edge[s]) + inside
                out_ref[s, inner, :] = (
                    second[s] + reacted(table_ref, next_at, second, s) - inside + kb * (p_ref[s, third_at, :] - second[s])
                )
        for n, plane in ((2, nz - 1), (3, nz - 2)) if top else ((0, 0), (1, 1)):
            copies.append(
                pltpu.make_async_copy(
                    out_ref.at[:, pl.ds(n * nx, nx), :], out_hbm.at[:, pl.ds(plane * nx, nx), :], sems.at[n]
                )
            )
            copies[-1].start()
    for copy in copies:
        copy.wait()


def involution(size, step):
    return [(i, i ^ step) for i in range(size)]


def halo_pairs(gx, gz, start):
    pairs = []
    for j in range(gz):
        partner = j + 1 if (j - start) % 2 == 0 else j - 1
        for i in range(gx):
            if 0 <= partner < gz:
                pairs.append((i * gz + j, i * gz + partner))
            else:
                pairs.append((i * gz + j, (i ^ 1) * gz + j))
    return pairs


def shards(concentration, facies, x_rates, y_rates, z_rates, react_table, gx, gz):
    species, nz, nx, ny = concentration.shape
    classes = x_rates.shape[0]
    dims = (species, nz, nx, ny, classes)
    axes = ("gx", "gz")
    rows = nz * nx
    half = ny // SUBS // 2
    f32 = jnp.float32
    shape = lambda *d: jax.ShapeDtypeStruct(d, f32)
    scratch = lambda *d: pltpu.VMEM(d, f32)
    dma = lambda n: pltpu.SemaphoreType.DMA((n,))

    def call(kernel, name, out_shape, in_specs, out_specs=None, scratch_shapes=(), **options):
        return pl.pallas_call(
            kernel,
            out_shape=out_shape,
            in_specs=in_specs,
            out_specs=out_specs or [VMEM] * len(out_shape),
            scratch_shapes=list(scratch_shapes),
            compiler_params=pltpu.CompilerParams(vmem_limit_bytes=8 << 20),
            name=name,
            **options,
        )

    in_hbm = lambda array: pltpu.with_memory_space_constraint(array, pltpu.HBM)
    react = jnp.transpose(react_table, (1, 2, 0))
    c = concentration.reshape(species, rows, ny)
    fac = facies.reshape(rows, ny)
    rounds = gx.bit_length() - 1
    assert gx == 1 << rounds and rounds > 0 and gz > 1 and nz >= 4
    count, few = 3 + 2 * species, 1 + species
    blocks = ny // LANES

    ends, rk, ra, h, ry, c, fac = call(
        functools.partial(eliminate_x, dims),
        "eliminate_x",
        [shape(count, nz, ny), shape(nx, nz, ny), shape(nx, nz, ny), shape(species, nx, nz, ny), shape(rows, ny),
         shape(species, rows, ny), jax.ShapeDtypeStruct((rows, ny), jnp.int32)],
        [HBM] * 4,
        scratch_shapes=[scratch(species, blocks, rows + nz, LANES), scratch(blocks, rows + nz, LANES), scratch(rows, ny),
                        pltpu.SMEM((classes,), f32), pltpu.SMEM((classes,), f32), dma(3 + species)],
    )(in_hbm(x_rates), in_hbm(y_rates), in_hbm(c), in_hbm(fac))

    y_fac = call(
        functools.partial(y_factors, dims),
        "y_factors",
        [shape(2, half, SUBS, rows)] * 3 + [shape(3 * (2 + len(sub_levels())), SUBS, rows)],
        [VMEM],
        scratch_shapes=[scratch(ny + SUBS, rows)],
    )(ry)
    kz, rz, table = call(
        functools.partial(z_tables, dims),
        "z_tables",
        [shape(rows - nx, ny), shape(rows, ny), shape(species * species, rows, ny)],
        [HBM, HBM, VMEM, ANY],
        scratch_shapes=[pltpu.SMEM((classes,), f32), pltpu.SMEM(react.shape, f32), dma(2)],
    )(in_hbm(z_rates), in_hbm(react), fac, ends)

    saved, own = [], ends
    side_work = [y_fac[3], table]
    for bit in range(rounds - 1):
        got = lax.ppermute(own, "gx", involution(gx, 1 << bit))
        final = bit == rounds - 2
        out_shape = [shape(few if final else count, nz, ny), shape(2 + species, nz, ny)] + [shape(few, nz, ny)] * final
        merged = call(
            functools.partial(merge_x, species, bit, final, "gx"), f"merge_x{bit}", out_shape, [VMEM, VMEM, ANY]
        )(own, got, side_work[min(bit, 1)])
        own = merged[0]
        saved.append(merged[1])
    if rounds > 1:
        outer = merged[2]
    else:
        own, outer = call(
            functools.partial(last_message, species, "gx"), "last_message", [shape(few, nz, ny)] * 2, [VMEM, ANY]
        )(own, table)
    got = lax.ppermute(own, "gx", involution(gx, 1 << (rounds - 1)))

    def solve(*refs):
        n = len(saved)
        solve_lines(dims, axes, list(range(rounds)), refs[0], refs[1], refs[2], refs[3 : 3 + n], *refs[3 + n :])

    operands = [own, got, outer] + saved + [rk, ra, h, c] + list(y_fac) + [kz, rz, table]
    m, to_a, to_b = call(
        solve,
        "solve_lines",
        [shape(species, rows, ny), shape(2 * species + 1, nx, ny), shape(2 * species + 1, nx, ny)],
        [VMEM] * len(operands),
        scratch_shapes=[scratch(species, blocks, rows + nz, LANES), scratch(species, ny + SUBS, rows)],
    )(*operands)

    got_a = lax.ppermute(to_a, axes, halo_pairs(gx, gz, 0))
    got_b = lax.ppermute(to_b, axes, halo_pairs(gx, gz, 1))
    p, inner = call(
        functools.partial(inner_passes, dims),
        "inner_passes",
        [shape(species, rows, ny)] * 2,
        [VMEM] * 3,
        [VMEM, HBM],
        scratch_shapes=[scratch(species, rows, ny), dma(nz - 4)],
    )(m, kz, table)
    (out,) = call(
        functools.partial(outer_passes, dims, axes, gz),
        "outer_passes",
        [shape(species, rows, ny)],
        [VMEM] * 7 + [HBM],
        [HBM],
        scratch_shapes=[scratch(species, 4 * nx, ny), dma(4)],
        input_output_aliases={7: 0},
    )(m, p, got_a, got_b, kz, rz, table, inner)
    return out.reshape(concentration.shape)


def solution(mesh):
    in_specs = (P(None, "gz", "gx", None), P("gz", "gx", None), P(), P(), P(), P())
    out_specs = P(None, "gz", "gx", None)
    body = functools.partial(shards, gx=mesh.shape["gx"], gz=mesh.shape["gz"])
    return jax.shard_map(body, mesh=mesh, in_specs=in_specs, out_specs=out_specs, check_vma=False)
```

```python
import functools
import jax
import jax.numpy as jnp
from jax import lax
from jax.experimental import pallas as pl
from jax.experimental.pallas import tpu as pltpu
from jax.sharding import PartitionSpec as P

PASSES = 2
LANES = 128
SUBS = 8

VMEM = pl.BlockSpec(memory_space=pltpu.VMEM)
ANY = pl.BlockSpec(memory_space=pl.ANY)
HBM = pl.BlockSpec(memory_space=pltpu.HBM)


def face(a, b):
    return 2.0 * a * b / (a + b)


def picked(table, masks):
    value = table(0)
    for index, mask in masks:
        value = jnp.where(mask, table(index), value)
    return value


def class_masks(facies, classes):
    return [(index, facies == index) for index in range(1, classes)]


def merge_blocks(left, right):
    g1, lp, lq = left
    g2, lm, ln = right
    leak = lq + lm
    r = 1.0 / (g1 + g2 + leak)
    before, after = g1 * r, g2 * r
    return (g1 * after, lp + before * leak, ln + after * leak), (r, before, after)


def apart(row, length):
    return pl.ds(row + row // length, SUBS)


def spread(ref, at, value):
    for lo in range(0, value.shape[1], LANES):
        ref[lo // LANES, at, :] = value[:, lo : lo + LANES]


def eliminate_x(dims, xr_hbm, yr_hbm, c_hbm, fac_hbm, ends_ref, rk_ref, ra_ref, h_ref, ry_ref, c_ref, fac_ref,
                e_ref, rx_ref, ky_ref, x_rates, y_rates, sems):
    species, nz, nx, ny, classes = dims
    rows = nz * nx
    copies = [
        pltpu.make_async_copy(fac_hbm, fac_ref, sems.at[0]),
        pltpu.make_async_copy(xr_hbm, x_rates, sems.at[1]),
        pltpu.make_async_copy(yr_hbm, y_rates, sems.at[2]),
    ]
    arrivals = [pltpu.make_async_copy(c_hbm.at[s], c_ref.at[s], sems.at[3 + s]) for s in range(species)]
    for copy in copies + arrivals:
        copy.start()
    lane = lax.broadcasted_iota(jnp.int32, (SUBS, ny), 1)
    not_last = lane < ny - 1
    for copy in copies:
        copy.wait()
    for row in range(0, rows, SUBS):
        at = pl.ds(row, SUBS)
        masks = class_masks(fac_ref[at, :], classes)
        spread(rx_ref, apart(row, nx), picked(lambda i: x_rates[i], masks))
        ry = picked(lambda i: y_rates[i], masks)
        ry_ref[at, :] = ry
        ky_ref[at, :] = jnp.where(not_last, face(ry, pltpu.roll(ry, ny - 1, 1)), 0.0)
    for s in range(species):
        arrivals[s].wait()
        for row in range(0, rows, SUBS):
            at = pl.ds(row, SUBS)
            c = c_ref[s, at, :]
            flux = ky_ref[at, :] * (pltpu.roll(c, ny - 1, 1) - c)
            spread(e_ref.at[s], apart(row, nx), c + (flux - pltpu.roll(flux, 1, 1)))
    for lo in range(0, ny, LANES):
        lanes = pl.ds(lo, LANES)
        row_at = [pl.ds(x, nz, stride=nx + 1) for x in range(nx)]
        rate = rx_ref[lo // LANES, row_at[0], :]
        a = 2.0 * rate
        excess = jnp.ones_like(a)
        leak = jnp.zeros_like(a)
        f = [e_ref[s, lo // LANES, row_at[0], :] for s in range(species)]
        first = [None] * species
        for x in range(nx):
            if x < nx - 1:
                rate_next = rx_ref[lo // LANES, row_at[x + 1], :]
                k = face(rate, rate_next)
                rate = rate_next
            else:
                k = 2.0 * rate
            r = 1.0 / (a + excess + k)
            rk, ra = k * r, a * r
            rk_ref[x, :, lanes] = rk
            ra_ref[x, :, lanes] = ra
            leak = leak + ra * excess
            a = a * rk
            excess = rk * excess
            if x < nx - 1:
                excess = 1.0 + excess
            for s in range(species):
                h_ref[s, x, :, lanes] = r * f[s]
                gain = ra * f[s]
                first[s] = gain if x == 0 else first[s] + gain
                f[s] = rk * f[s]
                if x < nx - 1:
                    f[s] = f[s] + e_ref[s, lo // LANES, row_at[x + 1], :]
        for i, value in enumerate([a, leak, excess] + first + f):
            ends_ref[i, :, lanes] = value


def side_of(axis, bit):
    return (lax.axis_index(axis) >> bit) & 1 == 1


def emit_block(final, next_side, block, fp, fn, lanes, out_ref, outer_ref):
    species = len(fp)
    if not final:
        for i, value in enumerate(list(block) + list(fp) + list(fn)):
            out_ref[i, :, lanes] = value
        return
    pick = lambda a, b: jnp.where(next_side, a, b)
    g, leak_p, leak_n = block
    leak_out, leak_in = pick(leak_n, leak_p), pick(leak_p, leak_n)
    r = 1.0 / (g + leak_out)
    share = g * r
    out_ref[0, :, lanes] = leak_in + share * leak_out
    outer_ref[0, :, lanes] = share
    for s in range(species):
        f_out, f_in = pick(fn[s], fp[s]), pick(fp[s], fn[s])
        out_ref[1 + s, :, lanes] = f_in + share * f_out
        outer_ref[1 + s, :, lanes] = r * f_out


def merge_x(species, bit, final, axis, own_ref, got_ref, after_ref, out_ref, saved_ref, outer_ref=None):
    side, next_side = side_of(axis, bit), side_of(axis, bit + 1)
    for lo in range(0, own_ref.shape[2], LANES):
        lanes = pl.ds(lo, LANES)
        own = [own_ref[i, :, lanes] for i in range(3 + 2 * species)]
        got = [got_ref[i, :, lanes] for i in range(3 + 2 * species)]
        left = [jnp.where(side, b, a) for a, b in zip(own, got)]
        right = [jnp.where(side, a, b) for a, b in zip(own, got)]
        block, (r, before, after) = merge_blocks(left[:3], right[:3])
        saved_ref[0, :, lanes] = before
        saved_ref[1, :, lanes] = after
        fp, fn = [], []
        for s in range(species):
            node = left[3 + species + s] + right[3 + s]
            fp.append(left[3 + s] + before * node)
            fn.append(right[3 + species + s] + after * node)
            saved_ref[2 + s, :, lanes] = r * node
        emit_block(final, next_side, block, fp, fn, lanes, out_ref, outer_ref)


def sub_levels():
    return [1 << n for n in range(SUBS.bit_length() - 1)]


def y_factors(dims, ry_ref, yr_ref, yk_ref, ya_ref, lv_ref, rt_ref):
    species, nz, nx, ny, classes = dims
    rows = nz * nx
    half = ny // SUBS // 2
    for lo in range(0, ny, LANES):
        turned = ry_ref[:, pl.ds(lo, LANES)].T
        for y in range(0, LANES, SUBS):
            rt_ref[apart(lo + y, 2 * half), :] = turned[y : y + SUBS]
    sub = lax.broadcasted_iota(jnp.int32, (SUBS, rows), 0)

    blocks = []
    for group in range(2):
        rates = [rt_ref[pl.ds(group * half + i, SUBS, stride=2 * half + 1), :] for i in range(half)]
        a = 2.0 * rates[0]
        excess = jnp.ones_like(a)
        leak = jnp.zeros_like(a)
        for i in range(half):
            k = face(rates[i], rates[i + 1]) if i < half - 1 else 2.0 * rates[i]
            r = 1.0 / (a + excess + k)
            rk, ra = k * r, a * r
            yr_ref[group, i] = r
            yk_ref[group, i] = rk
            ya_ref[group, i] = ra
            leak = leak + ra * excess
            a = a * rk
            excess = rk * excess
            if i < half - 1:
                excess = 1.0 + excess
        blocks.append((a, leak, excess))
    block, factors = merge_blocks(*blocks)
    kept = list(factors)
    for d in sub_levels():
        high = sub & d != 0
        from_low = [pltpu.roll(v, d, 0) for v in block]
        from_high = [pltpu.roll(v, SUBS - d, 0) for v in block]
        left = [jnp.where(high, b, a) for a, b in zip(block, from_low)]
        right = [jnp.where(high, a, b) for a, b in zip(block, from_high)]
        block, factors = merge_blocks(left, right)
        kept += list(factors)
    g, leak_p, leak_n = block
    rn = 1.0 / (g + leak_n)
    kept += [rn, g * rn, 1.0 / (leak_p + g * leak_n * rn)]
    for i, value in enumerate(kept):
        lv_ref[i] = value


def z_tables(dims, z_hbm, react_hbm, fac_ref, after_ref, kz_ref, rz_ref, table_ref, z_rates, react, sems):
    species, nz, nx, ny, classes = dims
    rows = nz * nx
    copies = [pltpu.make_async_copy(z_hbm, z_rates, sems.at[0]), pltpu.make_async_copy(react_hbm, react, sems.at[1])]
    for copy in copies:
        copy.start()
    for copy in copies:
        copy.wait()
    for row in range(0, rows, SUBS):
        at = pl.ds(row, SUBS)
        masks = class_masks(fac_ref[at, :], classes)
        rz_ref[at, :] = picked(lambda i: z_rates[i], masks)
        for t in range(species):
            for s in range(species):
                table_ref[t * species + s, at, :] = picked(lambda i: react[t, s, i], masks)
    for row in range(0, rows - nx, SUBS):
        kz_ref[pl.ds(row, SUBS), :] = face(rz_ref[pl.ds(row, SUBS), :], rz_ref[pl.ds(row + nx, SUBS), :])


def reacted(table_ref, at, amounts, t):
    species = len(amounts)
    total = table_ref[t * species, at, :] * amounts[0]
    for s in range(1, species):
        total = total + table_ref[t * species + s, at, :] * amounts[s]
    return total


def solve_lines(dims, axes, bits, own_ref, got_ref, outer_ref, saved_refs, rk_ref, ra_ref, h_ref, c_ref,
                yr_ref, yk_ref, ya_ref, lv_ref, kz_ref, rz_ref, table_ref,
                m_ref, up_ref, down_ref, u_ref, vt_ref):
    species, nz, nx, ny, classes = dims
    rows = nz * nx
    half = ny // SUBS // 2
    index = lax.axis_index(axes[0])
    sides = [(index >> bit) & 1 == 1 for bit in bits]
    for lo in range(0, ny, LANES):
        lanes = pl.ds(lo, LANES)
        inv = 1.0 / (own_ref[0, :, lanes] + got_ref[0, :, lanes])
        outer_share = outer_ref[0, :, lanes]
        level = [(saved[0, :, lanes], saved[1, :, lanes]) for saved in saved_refs]
        for s in range(species):
            inner = (own_ref[1 + s, :, lanes] + got_ref[1 + s, :, lanes]) * inv
            outer = outer_ref[1 + s, :, lanes] + outer_share * inner
            first = jnp.where(sides[-1], inner, outer)
            last = jnp.where(sides[-1], outer, inner)
            for n in reversed(range(len(saved_refs))):
                before, after = level[n]
                node = saved_refs[n][2 + s, :, lanes] + before * first + after * last
                first, last = jnp.where(sides[n], node, first), jnp.where(sides[n], last, node)
            value = last
            for x in reversed(range(nx)):
                value = h_ref[s, x, :, lanes] + ra_ref[x, :, lanes] * first + rk_ref[x, :, lanes] * value
                u_ref[s, lo // LANES, pl.ds(x, nz, stride=nx + 1), :] = value
    for s in range(species):
        for lo in range(0, ny, LANES):
            lanes = pl.ds(lo, LANES)
            pieces = [
                u_ref[s, lo // LANES, apart(row, nx), :] - c_ref[s, pl.ds(row, SUBS), lanes]
                for row in range(0, rows, SUBS)
            ]
            turned = jnp.concatenate(pieces, axis=0).T
            for y in range(0, LANES, SUBS):
                vt_ref[s, apart(lo + y, 2 * half), :] = turned[y : y + SUBS]

    def at_step(group, i):
        return pl.ds(group * half + i, SUBS, stride=2 * half + 1)

    sub = lax.broadcasted_iota(jnp.int32, (SUBS, rows), 0)
    ends = []
    for group in range(2):
        f = [vt_ref[s, at_step(group, 0), :] for s in range(species)]
        first = [None] * species
        for i in range(half):
            rk, ra = yk_ref[group, i], ya_ref[group, i]
            for s in range(species):
                gain = ra * f[s]
                first[s] = gain if i == 0 else first[s] + gain
                if i > 0:
                    vt_ref[s, at_step(group, i), :] = f[s]
                f[s] = rk * f[s]
                if i < half - 1:
                    f[s] = f[s] + vt_ref[s, at_step(group, i + 1), :]
        ends.append((first, f))
    levels = sub_levels()
    highs = [sub & d != 0 for d in levels]
    factors = [[lv_ref[3 * n + i] for i in range(3)] for n in range(len(levels) + 2)]
    solved = []
    for s in range(species):
        r, before, after = factors[0]
        node = ends[0][1][s] + ends[1][0][s]
        fp, fn = ends[0][0][s] + before * node, ends[1][1][s] + after * node
        kept = [r * node]
        for n, d in enumerate(levels):
            r, before, after = factors[n + 1]
            node = jnp.where(highs[n], fp + pltpu.roll(fn, d, 0), fn + pltpu.roll(fp, SUBS - d, 0))
            fp, fn = (
                jnp.where(highs[n], pltpu.roll(fp, d, 0), fp) + before * node,
                jnp.where(highs[n], fn, pltpu.roll(fn, SUBS - d, 0)) + after * node,
            )
            kept.append(r * node)
        rn, share, rp = factors[-1]
        first = (fp + share * fn) * rp
        last = rn * fn + share * first
        for n in reversed(range(len(levels))):
            r, before, after = factors[n + 1]
            node = kept[n + 1] + before * first + after * last
            first, last = jnp.where(highs[n], node, first), jnp.where(highs[n], last, node)
        r, before, after = factors[0]
        node = kept[0] + before * first + after * last
        solved.append(((first, node), (node, last)))
    for group in range(2):
        value = [solved[s][group][1] for s in range(species)]
        for i in reversed(range(half)):
            r, rk, ra = yr_ref[group, i], yk_ref[group, i], ya_ref[group, i]
            for s in range(species):
                value[s] = r * vt_ref[s, at_step(group, i), :] + ra * solved[s][group][0] + rk * value[s]
                vt_ref[s, at_step(group, i), :] = value[s]
    for s in range(species):
        for lo in range(0, ny, LANES):
            lanes = pl.ds(lo, LANES)
            pieces = [vt_ref[s, apart(lo + y, 2 * half), :] for y in range(0, LANES, SUBS)]
            m_ref[s, :, lanes] = c_ref[s, :, lanes] + 2.0 * jnp.concatenate(pieces, axis=0).T
    odd = lax.axis_index(axes[1]) & 1 == 1
    for part in range(0, nx, SUBS):
        here = pl.ds(part, SUBS)
        top, below_top = pl.ds(rows - nx + part, SUBS), pl.ds(rows - 2 * nx + part, SUBS)
        low, above_low = pl.ds(part, SUBS), pl.ds(nx + part, SUBS)
        m_top = [m_ref[s, top, :] for s in range(species)]
        m_low = [m_ref[s, low, :] for s in range(species)]
        k_top, k_low = kz_ref[below_top, :], kz_ref[low, :]
        for s in range(species):
            q_top = m_top[s] + reacted(table_ref, top, m_top, s) - k_top * (m_top[s] - m_ref[s, below_top, :])
            q_low = m_low[s] + reacted(table_ref, low, m_low, s) + k_low * (m_ref[s, above_low, :] - m_low[s])
            for n, (t, l) in enumerate(((m_top[s], m_low[s]), (q_top, q_low))):
                up_ref[n * species + s, here, :] = jnp.where(odd, l, t)
                down_ref[n * species + s, here, :] = jnp.where(odd, t, l)
        up_ref[2 * species, here, :] = jnp.where(odd, rz_ref[low, :], rz_ref[top, :])
        down_ref[2 * species, here, :] = jnp.where(odd, rz_ref[top, :], rz_ref[low, :])


def inner_passes(dims, m_ref, kz_ref, table_ref, p_ref, base_ref, out_hbm, sems):
    species, nz, nx, ny, classes = dims

    def one_pass(source, target, z):
        for part in range(0, nx, SUBS):
            row = z * nx + part
            at = pl.ds(row, SUBS)
            amounts = [source[s, at, :] for s in range(species)]
            for s in range(species):
                total = amounts[s] + reacted(table_ref, at, amounts, s)
                if z < nz - 1:
                    total = total + kz_ref[at, :] * (source[s, pl.ds(row + nx, SUBS), :] - amounts[s])
                if z > 0:
                    total = total - kz_ref[pl.ds(row - nx, SUBS), :] * (amounts[s] - source[s, pl.ds(row - nx, SUBS), :])
                target[s, at, :] = total

    copies = []
    for z in range(nz + 1):
        if z < nz:
            one_pass(m_ref, p_ref, z)
        if z == 0:
            continue
        one_pass(p_ref, base_ref, z - 1)
        if 2 <= z - 1 < nz - 2:
            planes = pl.ds((z - 1) * nx, nx)
            copies.append(pltpu.make_async_copy(base_ref.at[:, planes, :], out_hbm.at[:, planes, :], sems.at[len(copies)]))
            copies[-1].start()
    for copy in copies:
        copy.wait()


def outer_side(dims, axis, planes, start, m_ref, p_ref, base_ref, got_ref, kz_ref, rz_ref, table_ref, part_hbm, out_hbm,
               edge_ref, next_ref, sems):
    species, nz, nx, ny, classes = dims
    place = lax.axis_index(axis)
    top = (place + start) & 1 == 0
    exists = jnp.where(top, place < planes - 1, place > 0)
    rows_of = lambda up, low: pl.multiple_of(jnp.where(top, up * nx, low * nx), SUBS)
    edge_row, next_row, face_row = rows_of(nz - 1, 0), rows_of(nz - 2, 1), rows_of(nz - 2, 0)
    for part in range(0, nx, SUBS):
        here = pl.ds(part, SUBS)
        at, next_at = pl.ds(edge_row + part, SUBS), pl.ds(next_row + part, SUBS)
        k = jnp.where(exists, face(rz_ref[at, :], got_ref[2 * species, here, :]), 0.0)
        inside = kz_ref[pl.ds(face_row + part, SUBS), :]
        flux = [k * (got_ref[s, here, :] - m_ref[s, at, :]) for s in range(species)]
        for s in range(species):
            across = inside * flux[s]
            next_ref[s, here, :] = base_ref[s, next_at, :] + across
            difference = got_ref[species + s, here, :] - flux[s] - (p_ref[s, at, :] + flux[s])
            edge_ref[s, here, :] = (
                base_ref[s, at, :] + flux[s] - across + reacted(table_ref, at, flux, s) + k * difference
            )
    copies = [
        pltpu.make_async_copy(next_ref, out_hbm.at[:, pl.ds(next_row, nx), :], sems.at[0]),
        pltpu.make_async_copy(edge_ref, out_hbm.at[:, pl.ds(edge_row, nx), :], sems.at[1]),
    ]
    for copy in copies:
        copy.start()
    for copy in copies:
        copy.wait()


def involution(size, step):
    return [(i, i ^ step) for i in range(size)]


def halo_pairs(gx, gz, start):
    pairs = []
    for j in range(gz):
        partner = j + 1 if (j - start) % 2 == 0 else j - 1
        for i in range(gx):
            if 0 <= partner < gz:
                pairs.append((i * gz + j, i * gz + partner))
            else:
                pairs.append((i * gz + j, (i ^ 1) * gz + j))
    return pairs


def shards(concentration, facies, x_rates, y_rates, z_rates, react_table, gx, gz):
    species, nz, nx, ny = concentration.shape
    classes = x_rates.shape[0]
    dims = (species, nz, nx, ny, classes)
    axes = ("gx", "gz")
    rows = nz * nx
    half = ny // SUBS // 2
    f32 = jnp.float32
    shape = lambda *d: jax.ShapeDtypeStruct(d, f32)
    scratch = lambda *d: pltpu.VMEM(d, f32)
    dma = lambda n: pltpu.SemaphoreType.DMA((n,))

    def call(kernel, name, out_shape, in_specs, out_specs=None, scratch_shapes=(), **options):
        return pl.pallas_call(
            kernel,
            out_shape=out_shape,
            in_specs=in_specs,
            out_specs=out_specs or [VMEM] * len(out_shape),
            scratch_shapes=list(scratch_shapes),
            compiler_params=pltpu.CompilerParams(vmem_limit_bytes=8 << 20),
            name=name,
            **options,
        )

    in_hbm = lambda array: pltpu.with_memory_space_constraint(array, pltpu.HBM)
    react = jnp.transpose(react_table, (1, 2, 0))
    c = concentration.reshape(species, rows, ny)
    fac = facies.reshape(rows, ny)
    rounds = gx.bit_length() - 1
    assert gx == 1 << rounds and rounds > 2 and gz > 1 and nz > 4
    count, few = 3 + 2 * species, 1 + species
    blocks = ny // LANES

    ends, rk, ra, h, ry, c, fac = call(
        functools.partial(eliminate_x, dims),
        "eliminate_x",
        [shape(count, nz, ny), shape(nx, nz, ny), shape(nx, nz, ny), shape(species, nx, nz, ny), shape(rows, ny),
         shape(species, rows, ny), jax.ShapeDtypeStruct((rows, ny), jnp.int32)],
        [HBM] * 4,
        scratch_shapes=[scratch(species, blocks, rows + nz, LANES), scratch(blocks, rows + nz, LANES), scratch(rows, ny),
                        pltpu.SMEM((classes,), f32), pltpu.SMEM((classes,), f32), dma(3 + species)],
    )(in_hbm(x_rates), in_hbm(y_rates), in_hbm(c), in_hbm(fac))

    y_fac = call(
        functools.partial(y_factors, dims),
        "y_factors",
        [shape(2, half, SUBS, rows)] * 3 + [shape(3 * (2 + len(sub_levels())), SUBS, rows)],
        [VMEM],
        scratch_shapes=[scratch(ny + SUBS, rows)],
    )(ry)
    kz, rz, table = call(
        functools.partial(z_tables, dims),
        "z_tables",
        [shape(rows - nx, ny), shape(rows, ny), shape(species * species, rows, ny)],
        [HBM, HBM, VMEM, ANY],
        scratch_shapes=[pltpu.SMEM((classes,), f32), pltpu.SMEM(react.shape, f32), dma(2)],
    )(in_hbm(z_rates), in_hbm(react), fac, ends)

    saved, own = [], ends
    side_work = [y_fac[3], table]
    for bit in range(rounds - 1):
        got = lax.ppermute(own, "gx", involution(gx, 1 << bit))
        final = bit == rounds - 2
        out_shape = [shape(few if final else count, nz, ny), shape(2 + species, nz, ny)] + [shape(few, nz, ny)] * final
        merged = call(
            functools.partial(merge_x, species, bit, final, "gx"), f"merge_x{bit}", out_shape, [VMEM, VMEM, ANY]
        )(own, got, side_work[min(bit, 1)])
        own = merged[0]
        saved.append(merged[1])
    outer = merged[2]
    got = lax.ppermute(own, "gx", involution(gx, 1 << (rounds - 1)))

    def solve(*refs):
        n = len(saved)
        solve_lines(dims, axes, list(range(rounds)), refs[0], refs[1], refs[2], refs[3 : 3 + n], *refs[3 + n :])

    operands = [own, got, outer] + saved + [rk, ra, h, c] + list(y_fac) + [kz, rz, table]
    m, to_a, to_b = call(
        solve,
        "solve_lines",
        [shape(species, rows, ny), shape(2 * species + 1, nx, ny), shape(2 * species + 1, nx, ny)],
        [VMEM] * len(operands),
        scratch_shapes=[scratch(species, blocks, rows + nz, LANES), scratch(species, ny + SUBS, rows)],
    )(*operands)

    got_a = lax.ppermute(to_a, axes, halo_pairs(gx, gz, 0))
    got_b = lax.ppermute(to_b, axes, halo_pairs(gx, gz, 1))
    p, base, out = call(
        functools.partial(inner_passes, dims),
        "inner_passes",
        [shape(species, rows, ny)] * 3,
        [VMEM] * 3,
        [VMEM, VMEM, HBM],
        scratch_shapes=[dma(nz - 4)],
    )(m, kz, table)
    for start, got in ((0, got_a), (1, got_b)):
        (out,) = call(
            functools.partial(outer_side, dims, "gz", gz, start),
            f"outer_side{start}",
            [shape(species, rows, ny)],
            [VMEM] * 7 + [HBM],
            [HBM],
            scratch_shapes=[scratch(species, nx, ny), scratch(species, nx, ny), dma(2)],
            input_output_aliases={7: 0},
        )(m, p, base, got, kz, rz, table, out)
    return out.reshape(concentration.shape)


def solution(mesh):
    in_specs = (P(None, "gz", "gx", None), P("gz", "gx", None), P(), P(), P(), P())
    out_specs = P(None, "gz", "gx", None)
    body = functools.partial(shards, gx=mesh.shape["gx"], gz=mesh.shape["gz"])
    return jax.shard_map(body, mesh=mesh, in_specs=in_specs, out_specs=out_specs, check_vma=False)
```

```python
import functools
import jax
import jax.numpy as jnp
from jax import lax
from jax.experimental import pallas as pl
from jax.experimental.pallas import tpu as pltpu
from jax.sharding import PartitionSpec as P

PASSES = 2
LANES = 128
SUBS = 8

VMEM = pl.BlockSpec(memory_space=pltpu.VMEM)
ANY = pl.BlockSpec(memory_space=pl.ANY)
HBM = pl.BlockSpec(memory_space=pltpu.HBM)


def face(a, b):
    return 2.0 * a * b / (a + b)


def picked(table, masks):
    value = table(0)
    for index, mask in masks:
        value = jnp.where(mask, table(index), value)
    return value


def class_masks(facies, classes):
    return [(index, facies == index) for index in range(1, classes)]


def merge_blocks(left, right):
    g1, lp, lq = left
    g2, lm, ln = right
    leak = lq + lm
    r = 1.0 / (g1 + g2 + leak)
    before, after = g1 * r, g2 * r
    return (g1 * after, lp + before * leak, ln + after * leak), (r, before, after)


def apart(row, length):
    return pl.ds(row + row // length, SUBS)


def spread(ref, at, value):
    for lo in range(0, value.shape[1], LANES):
        ref[lo // LANES, at, :] = value[:, lo : lo + LANES]


def eliminate_x(dims, xr_hbm, yr_hbm, c_hbm, fac_hbm, ends_ref, rk_ref, ra_ref, h_ref, ry_ref, c_ref, fac_ref,
                e_ref, rx_ref, ky_ref, r_ref, x_rates, y_rates, sems):
    species, nz, nx, ny, classes = dims
    rows = nz * nx
    copies = [
        pltpu.make_async_copy(fac_hbm, fac_ref, sems.at[0]),
        pltpu.make_async_copy(xr_hbm, x_rates, sems.at[1]),
        pltpu.make_async_copy(yr_hbm, y_rates, sems.at[2]),
    ]
    arrivals = [pltpu.make_async_copy(c_hbm.at[s], c_ref.at[s], sems.at[3 + s]) for s in range(species)]
    for copy in copies + arrivals:
        copy.start()
    lane = lax.broadcasted_iota(jnp.int32, (SUBS, ny), 1)
    not_last = lane < ny - 1
    for copy in copies:
        copy.wait()
    for row in range(0, rows, SUBS):
        at = pl.ds(row, SUBS)
        masks = class_masks(fac_ref[at, :], classes)
        spread(rx_ref, apart(row, nx), picked(lambda i: x_rates[i], masks))
        ry = picked(lambda i: y_rates[i], masks)
        ry_ref[at, :] = ry
        ky_ref[at, :] = jnp.where(not_last, face(ry, pltpu.roll(ry, ny - 1, 1)), 0.0)
    row_at = [pl.ds(x, nz, stride=nx + 1) for x in range(nx)]

    def explicit(s, row):
        at = pl.ds(row, SUBS)
        c = c_ref[s, at, :]
        flux = ky_ref[at, :] * (pltpu.roll(c, ny - 1, 1) - c)
        spread(e_ref.at[s], apart(row, nx), c + (flux - pltpu.roll(flux, 1, 1)))

    def coefficients(block):
        lanes = pl.ds(block * LANES, LANES)
        rate = rx_ref[block, row_at[0], :]
        a = 2.0 * rate
        excess = jnp.ones_like(a)
        leak = jnp.zeros_like(a)
        for x in range(nx):
            if x < nx - 1:
                rate_next = rx_ref[block, row_at[x + 1], :]
                k = face(rate, rate_next)
                rate = rate_next
            else:
                k = 2.0 * rate
            r = 1.0 / (a + excess + k)
            rk, ra = k * r, a * r
            r_ref[x, :, lanes] = r
            rk_ref[x, :, lanes] = rk
            ra_ref[x, :, lanes] = ra
            leak = leak + ra * excess
            a = a * rk
            excess = rk * excess
            if x < nx - 1:
                excess = 1.0 + excess
        for i, value in enumerate([a, leak, excess]):
            ends_ref[i, :, lanes] = value

    def sources(which, block):
        lanes = pl.ds(block * LANES, LANES)
        f = {s: e_ref[s, block, row_at[0], :] for s in which}
        first = {}
        for x in range(nx):
            r, rk, ra = r_ref[x, :, lanes], rk_ref[x, :, lanes], ra_ref[x, :, lanes]
            for s in which:
                h_ref[s, x, :, lanes] = r * f[s]
                gain = ra * f[s]
                first[s] = gain if x == 0 else first[s] + gain
                f[s] = rk * f[s]
                if x < nx - 1:
                    f[s] = f[s] + e_ref[s, block, row_at[x + 1], :]
        for s in which:
            ends_ref[3 + s, :, lanes] = first[s]
            ends_ref[3 + species + s, :, lanes] = f[s]

    blocks = range(ny // LANES)
    for s in range(species):
        arrivals[s].wait()
        for row in range(0, rows, SUBS):
            explicit(s, row)
        for block in blocks:
            if s == 0:
                coefficients(block)
            elif s == species // 2:
                sources(range(s), block)
    for block in blocks:
        sources(range(species // 2, species), block)


def side_of(axis, bit):
    return (lax.axis_index(axis) >> bit) & 1 == 1


def emit_block(final, next_side, block, fp, fn, lanes, out_ref, outer_ref):
    species = len(fp)
    if not final:
        for i, value in enumerate(list(block) + list(fp) + list(fn)):
            out_ref[i, :, lanes] = value
        return
    pick = lambda a, b: jnp.where(next_side, a, b)
    g, leak_p, leak_n = block
    leak_out, leak_in = pick(leak_n, leak_p), pick(leak_p, leak_n)
    r = 1.0 / (g + leak_out)
    share = g * r
    out_ref[0, :, lanes] = leak_in + share * leak_out
    outer_ref[0, :, lanes] = share
    for s in range(species):
        f_out, f_in = pick(fn[s], fp[s]), pick(fp[s], fn[s])
        out_ref[1 + s, :, lanes] = f_in + share * f_out
        outer_ref[1 + s, :, lanes] = r * f_out


def merge_x(species, bit, final, axes, own_ref, got_ref, after_ref, out_ref, saved_ref, outer_ref=None, *rate_refs):
    side, next_side = side_of(axes[0], bit), side_of(axes[0], bit + 1)
    if final:
        odd = side_of(axes[1], 0)
        nx = rate_refs[0].shape[0]
        low, top = after_ref[pl.ds(0, nx), :], after_ref[pl.ds(after_ref.shape[0] - nx, nx), :]
        rate_refs[0][...] = jnp.where(odd, low, top)
        rate_refs[1][...] = jnp.where(odd, top, low)
    for lo in range(0, own_ref.shape[2], LANES):
        lanes = pl.ds(lo, LANES)
        own = [own_ref[i, :, lanes] for i in range(3 + 2 * species)]
        got = [got_ref[i, :, lanes] for i in range(3 + 2 * species)]
        left = [jnp.where(side, b, a) for a, b in zip(own, got)]
        right = [jnp.where(side, a, b) for a, b in zip(own, got)]
        block, (r, before, after) = merge_blocks(left[:3], right[:3])
        saved_ref[0, :, lanes] = before
        saved_ref[1, :, lanes] = after
        fp, fn = [], []
        for s in range(species):
            node = left[3 + species + s] + right[3 + s]
            fp.append(left[3 + s] + before * node)
            fn.append(right[3 + species + s] + after * node)
            saved_ref[2 + s, :, lanes] = r * node
        emit_block(final, next_side, block, fp, fn, lanes, out_ref, outer_ref)


def sub_levels():
    return [1 << n for n in range(SUBS.bit_length() - 1)]


def y_factors(dims, ry_ref, yr_ref, yk_ref, ya_ref, lv_ref, rt_ref):
    species, nz, nx, ny, classes = dims
    rows = nz * nx
    half = ny // SUBS // 2
    for lo in range(0, ny, LANES):
        turned = ry_ref[:, pl.ds(lo, LANES)].T
        for y in range(0, LANES, SUBS):
            rt_ref[apart(lo + y, 2 * half), :] = turned[y : y + SUBS]
    sub = lax.broadcasted_iota(jnp.int32, (SUBS, rows), 0)

    blocks = []
    for group in range(2):
        rates = [rt_ref[pl.ds(group * half + i, SUBS, stride=2 * half + 1), :] for i in range(half)]
        a = 2.0 * rates[0]
        excess = jnp.ones_like(a)
        leak = jnp.zeros_like(a)
        for i in range(half):
            k = face(rates[i], rates[i + 1]) if i < half - 1 else 2.0 * rates[i]
            r = 1.0 / (a + excess + k)
            rk, ra = k * r, a * r
            yr_ref[group, i] = r
            yk_ref[group, i] = rk
            ya_ref[group, i] = ra
            leak = leak + ra * excess
            a = a * rk
            excess = rk * excess
            if i < half - 1:
                excess = 1.0 + excess
        blocks.append((a, leak, excess))
    block, factors = merge_blocks(*blocks)
    kept = list(factors)
    for d in sub_levels():
        high = sub & d != 0
        from_low = [pltpu.roll(v, d, 0) for v in block]
        from_high = [pltpu.roll(v, SUBS - d, 0) for v in block]
        left = [jnp.where(high, b, a) for a, b in zip(block, from_low)]
        right = [jnp.where(high, a, b) for a, b in zip(block, from_high)]
        block, factors = merge_blocks(left, right)
        kept += list(factors)
    g, leak_p, leak_n = block
    rn = 1.0 / (g + leak_n)
    kept += [rn, g * rn, 1.0 / (leak_p + g * leak_n * rn)]
    for i, value in enumerate(kept):
        lv_ref[i] = value


def z_tables(dims, z_hbm, react_hbm, fac_ref, after_ref, kz_ref, rz_ref, table_ref, z_rates, react, sems):
    species, nz, nx, ny, classes = dims
    rows = nz * nx
    copies = [pltpu.make_async_copy(z_hbm, z_rates, sems.at[0]), pltpu.make_async_copy(react_hbm, react, sems.at[1])]
    for copy in copies:
        copy.start()
    for copy in copies:
        copy.wait()
    for row in range(0, rows, SUBS):
        at = pl.ds(row, SUBS)
        masks = class_masks(fac_ref[at, :], classes)
        rz_ref[at, :] = picked(lambda i: z_rates[i], masks)
        for t in range(species):
            for s in range(species):
                table_ref[t * species + s, at, :] = picked(lambda i: react[t, s, i], masks)
    for row in range(0, rows - nx, SUBS):
        kz_ref[pl.ds(row, SUBS), :] = face(rz_ref[pl.ds(row, SUBS), :], rz_ref[pl.ds(row + nx, SUBS), :])


def reacted(table_ref, at, amounts, t):
    species = len(amounts)
    total = table_ref[t * species, at, :] * amounts[0]
    for s in range(1, species):
        total = total + table_ref[t * species + s, at, :] * amounts[s]
    return total


def solve_lines(dims, axes, bits, own_ref, got_ref, outer_ref, saved_refs, rk_ref, ra_ref, h_ref, c_ref,
                yr_ref, yk_ref, ya_ref, lv_ref, kz_ref, table_ref,
                m_ref, up_ref, down_ref, u_ref, vt_ref):
    species, nz, nx, ny, classes = dims
    rows = nz * nx
    half = ny // SUBS // 2
    index = lax.axis_index(axes[0])
    sides = [(index >> bit) & 1 == 1 for bit in bits]
    for lo in range(0, ny, LANES):
        lanes = pl.ds(lo, LANES)
        inv = 1.0 / (own_ref[0, :, lanes] + got_ref[0, :, lanes])
        outer_share = outer_ref[0, :, lanes]
        level = [(saved[0, :, lanes], saved[1, :, lanes]) for saved in saved_refs]
        for s in range(species):
            inner = (own_ref[1 + s, :, lanes] + got_ref[1 + s, :, lanes]) * inv
            outer = outer_ref[1 + s, :, lanes] + outer_share * inner
            first = jnp.where(sides[-1], inner, outer)
            last = jnp.where(sides[-1], outer, inner)
            for n in reversed(range(len(saved_refs))):
                before, after = level[n]
                node = saved_refs[n][2 + s, :, lanes] + before * first + after * last
                first, last = jnp.where(sides[n], node, first), jnp.where(sides[n], last, node)
            value = last
            for x in reversed(range(nx)):
                value = h_ref[s, x, :, lanes] + ra_ref[x, :, lanes] * first + rk_ref[x, :, lanes] * value
                u_ref[s, lo // LANES, pl.ds(x, nz, stride=nx + 1), :] = value
    for s in range(species):
        for lo in range(0, ny, LANES):
            lanes = pl.ds(lo, LANES)
            pieces = [
                u_ref[s, lo // LANES, apart(row, nx), :] - c_ref[s, pl.ds(row, SUBS), lanes]
                for row in range(0, rows, SUBS)
            ]
            turned = jnp.concatenate(pieces, axis=0).T
            for y in range(0, LANES, SUBS):
                vt_ref[s, apart(lo + y, 2 * half), :] = turned[y : y + SUBS]

    def at_step(group, i):
        return pl.ds(group * half + i, SUBS, stride=2 * half + 1)

    sub = lax.broadcasted_iota(jnp.int32, (SUBS, rows), 0)
    ends = []
    for group in range(2):
        f = [vt_ref[s, at_step(group, 0), :] for s in range(species)]
        first = [None] * species
        for i in range(half):
            rk, ra = yk_ref[group, i], ya_ref[group, i]
            for s in range(species):
                gain = ra * f[s]
                first[s] = gain if i == 0 else first[s] + gain
                if i > 0:
                    vt_ref[s, at_step(group, i), :] = f[s]
                f[s] = rk * f[s]
                if i < half - 1:
                    f[s] = f[s] + vt_ref[s, at_step(group, i + 1), :]
        ends.append((first, f))
    levels = sub_levels()
    highs = [sub & d != 0 for d in levels]
    factors = [[lv_ref[3 * n + i] for i in range(3)] for n in range(len(levels) + 2)]
    solved = []
    for s in range(species):
        r, before, after = factors[0]
        node = ends[0][1][s] + ends[1][0][s]
        fp, fn = ends[0][0][s] + before * node, ends[1][1][s] + after * node
        kept = [r * node]
        for n, d in enumerate(levels):
            r, before, after = factors[n + 1]
            node = jnp.where(highs[n], fp + pltpu.roll(fn, d, 0), fn + pltpu.roll(fp, SUBS - d, 0))
            fp, fn = (
                jnp.where(highs[n], pltpu.roll(fp, d, 0), fp) + before * node,
                jnp.where(highs[n], fn, pltpu.roll(fn, SUBS - d, 0)) + after * node,
            )
            kept.append(r * node)
        rn, share, rp = factors[-1]
        first = (fp + share * fn) * rp
        last = rn * fn + share * first
        for n in reversed(range(len(levels))):
            r, before, after = factors[n + 1]
            node = kept[n + 1] + before * first + after * last
            first, last = jnp.where(highs[n], node, first), jnp.where(highs[n], last, node)
        r, before, after = factors[0]
        node = kept[0] + before * first + after * last
        solved.append(((first, node), (node, last)))
    for group in range(2):
        value = [solved[s][group][1] for s in range(species)]
        for i in reversed(range(half)):
            r, rk, ra = yr_ref[group, i], yk_ref[group, i], ya_ref[group, i]
            for s in range(species):
                value[s] = r * vt_ref[s, at_step(group, i), :] + ra * solved[s][group][0] + rk * value[s]
                vt_ref[s, at_step(group, i), :] = value[s]
    for s in range(species):
        for lo in range(0, ny, LANES):
            lanes = pl.ds(lo, LANES)
            pieces = [vt_ref[s, apart(lo + y, 2 * half), :] for y in range(0, LANES, SUBS)]
            m_ref[s, :, lanes] = c_ref[s, :, lanes] + 2.0 * jnp.concatenate(pieces, axis=0).T
    odd = lax.axis_index(axes[1]) & 1 == 1
    for part in range(0, nx, SUBS):
        here = pl.ds(part, SUBS)
        top, below_top = pl.ds(rows - nx + part, SUBS), pl.ds(rows - 2 * nx + part, SUBS)
        low, above_low = pl.ds(part, SUBS), pl.ds(nx + part, SUBS)
        m_top = [m_ref[s, top, :] for s in range(species)]
        m_low = [m_ref[s, low, :] for s in range(species)]
        k_top, k_low = kz_ref[below_top, :], kz_ref[low, :]
        for s in range(species):
            q_top = m_top[s] + reacted(table_ref, top, m_top, s) - k_top * (m_top[s] - m_ref[s, below_top, :])
            q_low = m_low[s] + reacted(table_ref, low, m_low, s) + k_low * (m_ref[s, above_low, :] - m_low[s])
            for n, (t, l) in enumerate(((m_top[s], m_low[s]), (q_top, q_low))):
                up_ref[n * species + s, here, :] = jnp.where(odd, l, t)
                down_ref[n * species + s, here, :] = jnp.where(odd, t, l)


def inner_passes(dims, m_ref, kz_ref, table_ref, p_ref, base_ref, out_hbm, sems):
    species, nz, nx, ny, classes = dims

    def one_pass(source, target, z):
        for part in range(0, nx, SUBS):
            row = z * nx + part
            at = pl.ds(row, SUBS)
            amounts = [source[s, at, :] for s in range(species)]
            for s in range(species):
                total = amounts[s] + reacted(table_ref, at, amounts, s)
                if z < nz - 1:
                    total = total + kz_ref[at, :] * (source[s, pl.ds(row + nx, SUBS), :] - amounts[s])
                if z > 0:
                    total = total - kz_ref[pl.ds(row - nx, SUBS), :] * (amounts[s] - source[s, pl.ds(row - nx, SUBS), :])
                target[s, at, :] = total

    copies = []
    for z in range(nz + 1):
        if z < nz:
            one_pass(m_ref, p_ref, z)
        if z == 0:
            continue
        one_pass(p_ref, base_ref, z - 1)
        if 2 <= z - 1 < nz - 2:
            planes = pl.ds((z - 1) * nx, nx)
            copies.append(pltpu.make_async_copy(base_ref.at[:, planes, :], out_hbm.at[:, planes, :], sems.at[len(copies)]))
            copies[-1].start()
    for copy in copies:
        copy.wait()


def outer_side(dims, axis, planes, start, m_ref, p_ref, base_ref, got_ref, rate_ref, kz_ref, rz_ref, table_ref, part_hbm, out_hbm,
               edge_ref, next_ref, sems):
    species, nz, nx, ny, classes = dims
    place = lax.axis_index(axis)
    top = (place + start) & 1 == 0
    exists = jnp.where(top, place < planes - 1, place > 0)
    rows_of = lambda up, low: pl.multiple_of(jnp.where(top, up * nx, low * nx), SUBS)
    edge_row, next_row, face_row = rows_of(nz - 1, 0), rows_of(nz - 2, 1), rows_of(nz - 2, 0)
    for part in range(0, nx, SUBS):
        here = pl.ds(part, SUBS)
        at, next_at = pl.ds(edge_row + part, SUBS), pl.ds(next_row + part, SUBS)
        k = jnp.where(exists, face(rz_ref[at, :], rate_ref[here, :]), 0.0)
        inside = kz_ref[pl.ds(face_row + part, SUBS), :]
        flux = [k * (got_ref[s, here, :] - m_ref[s, at, :]) for s in range(species)]
        for s in range(species):
            across = inside * flux[s]
            next_ref[s, here, :] = base_ref[s, next_at, :] + across
            difference = got_ref[species + s, here, :] - flux[s] - (p_ref[s, at, :] + flux[s])
            edge_ref[s, here, :] = (
                base_ref[s, at, :] + flux[s] - across + reacted(table_ref, at, flux, s) + k * difference
            )
    copies = [
        pltpu.make_async_copy(next_ref, out_hbm.at[:, pl.ds(next_row, nx), :], sems.at[0]),
        pltpu.make_async_copy(edge_ref, out_hbm.at[:, pl.ds(edge_row, nx), :], sems.at[1]),
    ]
    for copy in copies:
        copy.start()
    for copy in copies:
        copy.wait()


def involution(size, step):
    return [(i, i ^ step) for i in range(size)]


def halo_pairs(gx, gz, start):
    pairs = []
    for j in range(gz):
        partner = j + 1 if (j - start) % 2 == 0 else j - 1
        for i in range(gx):
            if 0 <= partner < gz:
                pairs.append((i * gz + j, i * gz + partner))
            else:
                pairs.append((i * gz + j, (i ^ 1) * gz + j))
    return pairs


def shards(concentration, facies, x_rates, y_rates, z_rates, react_table, gx, gz):
    species, nz, nx, ny = concentration.shape
    classes = x_rates.shape[0]
    dims = (species, nz, nx, ny, classes)
    axes = ("gx", "gz")
    rows = nz * nx
    half = ny // SUBS // 2
    f32 = jnp.float32
    shape = lambda *d: jax.ShapeDtypeStruct(d, f32)
    scratch = lambda *d: pltpu.VMEM(d, f32)
    dma = lambda n: pltpu.SemaphoreType.DMA((n,))

    def call(kernel, name, out_shape, in_specs, out_specs=None, scratch_shapes=(), **options):
        return pl.pallas_call(
            kernel,
            out_shape=out_shape,
            in_specs=in_specs,
            out_specs=out_specs or [VMEM] * len(out_shape),
            scratch_shapes=list(scratch_shapes),
            compiler_params=pltpu.CompilerParams(vmem_limit_bytes=8 << 20),
            name=name,
            **options,
        )

    in_hbm = lambda array: pltpu.with_memory_space_constraint(array, pltpu.HBM)
    react = jnp.transpose(react_table, (1, 2, 0))
    c = concentration.reshape(species, rows, ny)
    fac = facies.reshape(rows, ny)
    rounds = gx.bit_length() - 1
    assert gx == 1 << rounds and rounds > 2 and gz > 1 and nz > 4
    count, few = 3 + 2 * species, 1 + species
    blocks = ny // LANES

    ends, rk, ra, h, ry, c, fac = call(
        functools.partial(eliminate_x, dims),
        "eliminate_x",
        [shape(count, nz, ny), shape(nx, nz, ny), shape(nx, nz, ny), shape(species, nx, nz, ny), shape(rows, ny),
         shape(species, rows, ny), jax.ShapeDtypeStruct((rows, ny), jnp.int32)],
        [HBM] * 4,
        scratch_shapes=[scratch(species, blocks, rows + nz, LANES), scratch(blocks, rows + nz, LANES), scratch(rows, ny),
                        scratch(nx, nz, ny),
                        pltpu.SMEM((classes,), f32), pltpu.SMEM((classes,), f32), dma(3 + species)],
    )(in_hbm(x_rates), in_hbm(y_rates), in_hbm(c), in_hbm(fac))

    y_fac = call(
        functools.partial(y_factors, dims),
        "y_factors",
        [shape(2, half, SUBS, rows)] * 3 + [shape(3 * (2 + len(sub_levels())), SUBS, rows)],
        [VMEM],
        scratch_shapes=[scratch(ny + SUBS, rows)],
    )(ry)
    kz, rz, table = call(
        functools.partial(z_tables, dims),
        "z_tables",
        [shape(rows - nx, ny), shape(rows, ny), shape(species * species, rows, ny)],
        [HBM, HBM, VMEM, ANY],
        scratch_shapes=[pltpu.SMEM((classes,), f32), pltpu.SMEM(react.shape, f32), dma(2)],
    )(in_hbm(z_rates), in_hbm(react), fac, ends)

    saved, own = [], ends
    for bit in range(rounds - 1):
        got = lax.ppermute(own, "gx", involution(gx, 1 << bit))
        final = bit == rounds - 2
        out_shape = [shape(few if final else count, nz, ny), shape(2 + species, nz, ny)]
        out_shape += [shape(few, nz, ny), shape(nx, ny), shape(nx, ny)] * final
        merged = call(
            functools.partial(merge_x, species, bit, final, axes), f"merge_x{bit}", out_shape, [VMEM, VMEM, VMEM if final else ANY]
        )(own, got, rz if final else y_fac[3] if bit == 0 else table)
        own = merged[0]
        saved.append(merged[1])
    outer, rate_a, rate_b = merged[2:]
    got = lax.ppermute(own, "gx", involution(gx, 1 << (rounds - 1)))

    rate_a = lax.ppermute(rate_a, axes, halo_pairs(gx, gz, 0))
    rate_b = lax.ppermute(rate_b, axes, halo_pairs(gx, gz, 1))

    def solve(*refs):
        n = len(saved)
        solve_lines(dims, axes, list(range(rounds)), refs[0], refs[1], refs[2], refs[3 : 3 + n], *refs[3 + n :])

    operands = [own, got, outer] + saved + [rk, ra, h, c] + list(y_fac) + [kz, table]
    m, to_a, to_b = call(
        solve,
        "solve_lines",
        [shape(species, rows, ny), shape(2 * species, nx, ny), shape(2 * species, nx, ny)],
        [VMEM] * len(operands),
        scratch_shapes=[scratch(species, blocks, rows + nz, LANES), scratch(species, ny + SUBS, rows)],
    )(*operands)

    got_a = lax.ppermute(to_a, axes, halo_pairs(gx, gz, 0))
    got_b = lax.ppermute(to_b, axes, halo_pairs(gx, gz, 1))
    p, base, out = call(
        functools.partial(inner_passes, dims),
        "inner_passes",
        [shape(species, rows, ny)] * 3,
        [VMEM] * 3,
        [VMEM, VMEM, HBM],
        scratch_shapes=[dma(nz - 4)],
    )(m, kz, table)
    for start, got, rate in ((0, got_a, rate_a), (1, got_b, rate_b)):
        (out,) = call(
            functools.partial(outer_side, dims, "gz", gz, start),
            f"outer_side{start}",
            [shape(species, rows, ny)],
            [VMEM] * 8 + [HBM],
            [HBM],
            scratch_shapes=[scratch(species, nx, ny), scratch(species, nx, ny), dma(2)],
            input_output_aliases={8: 0},
        )(m, p, base, got, rate, kz, rz, table, out)
    return out.reshape(concentration.shape)


def solution(mesh):
    in_specs = (P(None, "gz", "gx", None), P("gz", "gx", None), P(), P(), P(), P())
    out_specs = P(None, "gz", "gx", None)
    body = functools.partial(shards, gx=mesh.shape["gx"], gz=mesh.shape["gz"])
    return jax.shard_map(body, mesh=mesh, in_specs=in_specs, out_specs=out_specs, check_vma=False)
```

```python
import functools
import jax
import jax.numpy as jnp
from jax import lax
from jax.experimental import pallas as pl
from jax.experimental.pallas import tpu as pltpu
from jax.sharding import PartitionSpec as P

LANES = 128
SUBS = 8

VMEM = pl.BlockSpec(memory_space=pltpu.VMEM)
ANY = pl.BlockSpec(memory_space=pl.ANY)
HBM = pl.BlockSpec(memory_space=pltpu.HBM)


def face(a, b):
    return 2.0 * a * b / (a + b)


def picked(table, masks):
    value = table(0)
    for index, mask in masks:
        value = jnp.where(mask, table(index), value)
    return value


def class_masks(facies, classes):
    return [(index, facies == index) for index in range(1, classes)]


def merge_blocks(left, right):
    g1, lp, lq = left
    g2, lm, ln = right
    leak = lq + lm
    r = 1.0 / (g1 + g2 + leak)
    before, after = g1 * r, g2 * r
    return (g1 * after, lp + before * leak, ln + after * leak), (r, before, after)


def apart(row, length):
    return pl.ds(row + row // length, SUBS)


def spread(ref, at, value):
    for lo in range(0, value.shape[1], LANES):
        ref[lo // LANES, at, :] = value[:, lo : lo + LANES]


def eliminate_x(dims, xr_hbm, yr_hbm, c_hbm, fac_hbm, ends_ref, rk_ref, ra_ref, h_ref, ry_ref, c_ref, fac_ref,
                e_ref, rx_ref, ky_ref, r_ref, x_rates, y_rates, sems):
    species, nz, nx, ny, classes = dims
    rows = nz * nx
    copies = [
        pltpu.make_async_copy(fac_hbm, fac_ref, sems.at[0]),
        pltpu.make_async_copy(xr_hbm, x_rates, sems.at[1]),
        pltpu.make_async_copy(yr_hbm, y_rates, sems.at[2]),
    ]
    arrivals = [pltpu.make_async_copy(c_hbm.at[s], c_ref.at[s], sems.at[3 + s]) for s in range(species)]
    for copy in copies + arrivals:
        copy.start()
    lane = lax.broadcasted_iota(jnp.int32, (SUBS, ny), 1)
    not_last = lane < ny - 1
    for copy in copies:
        copy.wait()
    for row in range(0, rows, SUBS):
        at = pl.ds(row, SUBS)
        masks = class_masks(fac_ref[at, :], classes)
        spread(rx_ref, apart(row, nx), picked(lambda i: x_rates[i], masks))
        ry = picked(lambda i: y_rates[i], masks)
        ry_ref[at, :] = ry
        ky_ref[at, :] = jnp.where(not_last, face(ry, pltpu.roll(ry, ny - 1, 1)), 0.0)
    row_at = [pl.ds(x, nz, stride=nx + 1) for x in range(nx)]

    def explicit(s, row):
        at = pl.ds(row, SUBS)
        c = c_ref[s, at, :]
        flux = ky_ref[at, :] * (pltpu.roll(c, ny - 1, 1) - c)
        spread(e_ref.at[s], apart(row, nx), c + (flux - pltpu.roll(flux, 1, 1)))

    def coefficients(block):
        lanes = pl.ds(block * LANES, LANES)
        rate = rx_ref[block, row_at[0], :]
        a = 2.0 * rate
        excess = jnp.ones_like(a)
        leak = jnp.zeros_like(a)
        for x in range(nx):
            if x < nx - 1:
                rate_next = rx_ref[block, row_at[x + 1], :]
                k = face(rate, rate_next)
                rate = rate_next
            else:
                k = 2.0 * rate
            r = 1.0 / (a + excess + k)
            rk, ra = k * r, a * r
            r_ref[x, :, lanes] = r
            rk_ref[x, :, lanes] = rk
            ra_ref[x, :, lanes] = ra
            leak = leak + ra * excess
            a = a * rk
            excess = rk * excess
            if x < nx - 1:
                excess = 1.0 + excess
        for i, value in enumerate([a, leak, excess]):
            ends_ref[i, :, lanes] = value

    def sources(which, block):
        lanes = pl.ds(block * LANES, LANES)
        f = {s: e_ref[s, block, row_at[0], :] for s in which}
        first = {}
        for x in range(nx):
            r, rk, ra = r_ref[x, :, lanes], rk_ref[x, :, lanes], ra_ref[x, :, lanes]
            for s in which:
                h_ref[s, x, :, lanes] = r * f[s]
                gain = ra * f[s]
                first[s] = gain if x == 0 else first[s] + gain
                f[s] = rk * f[s]
                if x < nx - 1:
                    f[s] = f[s] + e_ref[s, block, row_at[x + 1], :]
        for s in which:
            ends_ref[3 + s, :, lanes] = first[s]
            ends_ref[3 + species + s, :, lanes] = f[s]

    blocks = range(ny // LANES)
    for s in range(species):
        arrivals[s].wait()
        for row in range(0, rows, SUBS):
            explicit(s, row)
        for block in blocks:
            if s == 0:
                coefficients(block)
            elif s == species // 2:
                sources(range(s), block)
    for block in blocks:
        sources(range(species // 2, species), block)


def side_of(axis, bit):
    return (lax.axis_index(axis) >> bit) & 1 == 1


def emit_block(final, next_side, block, fp, fn, lanes, out_ref, outer_ref):
    species = len(fp)
    if not final:
        for i, value in enumerate(list(block) + list(fp) + list(fn)):
            out_ref[i, :, lanes] = value
        return
    pick = lambda a, b: jnp.where(next_side, a, b)
    g, leak_p, leak_n = block
    leak_out, leak_in = pick(leak_n, leak_p), pick(leak_p, leak_n)
    r = 1.0 / (g + leak_out)
    share = g * r
    out_ref[0, :, lanes] = leak_in + share * leak_out
    outer_ref[0, :, lanes] = share
    for s in range(species):
        f_out, f_in = pick(fn[s], fp[s]), pick(fp[s], fn[s])
        out_ref[1 + s, :, lanes] = f_in + share * f_out
        outer_ref[1 + s, :, lanes] = r * f_out


def merge_x(species, bit, final, axis, own_ref, got_ref, after_ref, out_ref, saved_ref, outer_ref=None):
    side, next_side = side_of(axis, bit), side_of(axis, bit + 1)
    for lo in range(0, own_ref.shape[2], LANES):
        lanes = pl.ds(lo, LANES)
        own = [own_ref[i, :, lanes] for i in range(3 + 2 * species)]
        got = [got_ref[i, :, lanes] for i in range(3 + 2 * species)]
        left = [jnp.where(side, b, a) for a, b in zip(own, got)]
        right = [jnp.where(side, a, b) for a, b in zip(own, got)]
        block, (r, before, after) = merge_blocks(left[:3], right[:3])
        saved_ref[0, :, lanes] = before
        saved_ref[1, :, lanes] = after
        fp, fn = [], []
        for s in range(species):
            node = left[3 + species + s] + right[3 + s]
            fp.append(left[3 + s] + before * node)
            fn.append(right[3 + species + s] + after * node)
            saved_ref[2 + s, :, lanes] = r * node
        emit_block(final, next_side, block, fp, fn, lanes, out_ref, outer_ref)


def sub_levels():
    return [1 << n for n in range(SUBS.bit_length() - 1)]


def y_factors(dims, ry_ref, yr_ref, yk_ref, ya_ref, lv_ref, rt_ref):
    _, nz, nx, ny, _ = dims
    rows = nz * nx
    half = ny // SUBS // 2
    for lo in range(0, ny, LANES):
        turned = ry_ref[:, pl.ds(lo, LANES)].T
        for y in range(0, LANES, SUBS):
            rt_ref[apart(lo + y, 2 * half), :] = turned[y : y + SUBS]
    sub = lax.broadcasted_iota(jnp.int32, (SUBS, rows), 0)

    blocks = []
    for group in range(2):
        rates = [rt_ref[pl.ds(group * half + i, SUBS, stride=2 * half + 1), :] for i in range(half)]
        a = 2.0 * rates[0]
        excess = jnp.ones_like(a)
        leak = jnp.zeros_like(a)
        for i in range(half):
            k = face(rates[i], rates[i + 1]) if i < half - 1 else 2.0 * rates[i]
            r = 1.0 / (a + excess + k)
            rk, ra = k * r, a * r
            yr_ref[group, i] = r
            yk_ref[group, i] = rk
            ya_ref[group, i] = ra
            leak = leak + ra * excess
            a = a * rk
            excess = rk * excess
            if i < half - 1:
                excess = 1.0 + excess
        blocks.append((a, leak, excess))
    block, factors = merge_blocks(*blocks)
    kept = list(factors)
    for d in sub_levels():
        high = sub & d != 0
        from_low = [pltpu.roll(v, d, 0) for v in block]
        from_high = [pltpu.roll(v, SUBS - d, 0) for v in block]
        left = [jnp.where(high, b, a) for a, b in zip(block, from_low)]
        right = [jnp.where(high, a, b) for a, b in zip(block, from_high)]
        block, factors = merge_blocks(left, right)
        kept += list(factors)
    g, leak_p, leak_n = block
    rn = 1.0 / (g + leak_n)
    kept += [rn, g * rn, 1.0 / (leak_p + g * leak_n * rn)]
    for i, value in enumerate(kept):
        lv_ref[i] = value


def z_tables(dims, z_hbm, react_hbm, fac_ref, after_ref, kz_ref, rz_ref, table_ref, z_rates, react, sems):
    species, nz, nx, _, classes = dims
    rows = nz * nx
    copies = [pltpu.make_async_copy(z_hbm, z_rates, sems.at[0]), pltpu.make_async_copy(react_hbm, react, sems.at[1])]
    for copy in copies:
        copy.start()
    for copy in copies:
        copy.wait()
    for row in range(0, rows, SUBS):
        at = pl.ds(row, SUBS)
        masks = class_masks(fac_ref[at, :], classes)
        rz_ref[at, :] = picked(lambda i: z_rates[i], masks)
        for t in range(species):
            for s in range(species):
                table_ref[t * species + s, at, :] = picked(lambda i: react[t, s, i], masks)
    for row in range(0, rows - nx, SUBS):
        kz_ref[pl.ds(row, SUBS), :] = face(rz_ref[pl.ds(row, SUBS), :], rz_ref[pl.ds(row + nx, SUBS), :])


def reacted(table_ref, at, amounts, t):
    species = len(amounts)
    total = table_ref[t * species, at, :] * amounts[0]
    for s in range(1, species):
        total = total + table_ref[t * species + s, at, :] * amounts[s]
    return total


def solve_lines(dims, axes, bits, own_ref, got_ref, outer_ref, saved_refs, rk_ref, ra_ref, h_ref, c_ref,
                yr_ref, yk_ref, ya_ref, lv_ref, kz_ref, rz_ref, table_ref,
                m_ref, up_ref, down_ref, u_ref, vt_ref):
    species, nz, nx, ny, _ = dims
    rows = nz * nx
    half = ny // SUBS // 2
    index = lax.axis_index(axes[0])
    sides = [(index >> bit) & 1 == 1 for bit in bits]
    for lo in range(0, ny, LANES):
        lanes = pl.ds(lo, LANES)
        inv = 1.0 / (own_ref[0, :, lanes] + got_ref[0, :, lanes])
        outer_share = outer_ref[0, :, lanes]
        level = [(saved[0, :, lanes], saved[1, :, lanes]) for saved in saved_refs]
        for s in range(species):
            inner = (own_ref[1 + s, :, lanes] + got_ref[1 + s, :, lanes]) * inv
            outer = outer_ref[1 + s, :, lanes] + outer_share * inner
            first = jnp.where(sides[-1], inner, outer)
            last = jnp.where(sides[-1], outer, inner)
            for n in reversed(range(len(saved_refs))):
                before, after = level[n]
                node = saved_refs[n][2 + s, :, lanes] + before * first + after * last
                first, last = jnp.where(sides[n], node, first), jnp.where(sides[n], last, node)
            value = last
            for x in reversed(range(nx)):
                value = h_ref[s, x, :, lanes] + ra_ref[x, :, lanes] * first + rk_ref[x, :, lanes] * value
                u_ref[s, lo // LANES, pl.ds(x, nz, stride=nx + 1), :] = value
    for s in range(species):
        for lo in range(0, ny, LANES):
            lanes = pl.ds(lo, LANES)
            pieces = [
                u_ref[s, lo // LANES, apart(row, nx), :] - c_ref[s, pl.ds(row, SUBS), lanes]
                for row in range(0, rows, SUBS)
            ]
            turned = jnp.concatenate(pieces, axis=0).T
            for y in range(0, LANES, SUBS):
                vt_ref[s, apart(lo + y, 2 * half), :] = turned[y : y + SUBS]

    def at_step(group, i):
        return pl.ds(group * half + i, SUBS, stride=2 * half + 1)

    sub = lax.broadcasted_iota(jnp.int32, (SUBS, rows), 0)
    ends = []
    for group in range(2):
        f = [vt_ref[s, at_step(group, 0), :] for s in range(species)]
        first = [None] * species
        for i in range(half):
            rk, ra = yk_ref[group, i], ya_ref[group, i]
            for s in range(species):
                gain = ra * f[s]
                first[s] = gain if i == 0 else first[s] + gain
                if i > 0:
                    vt_ref[s, at_step(group, i), :] = f[s]
                f[s] = rk * f[s]
                if i < half - 1:
                    f[s] = f[s] + vt_ref[s, at_step(group, i + 1), :]
        ends.append((first, f))
    levels = sub_levels()
    highs = [sub & d != 0 for d in levels]
    factors = [[lv_ref[3 * n + i] for i in range(3)] for n in range(len(levels) + 2)]
    solved = []
    for s in range(species):
        r, before, after = factors[0]
        node = ends[0][1][s] + ends[1][0][s]
        fp, fn = ends[0][0][s] + before * node, ends[1][1][s] + after * node
        kept = [r * node]
        for n, d in enumerate(levels):
            r, before, after = factors[n + 1]
            node = jnp.where(highs[n], fp + pltpu.roll(fn, d, 0), fn + pltpu.roll(fp, SUBS - d, 0))
            fp, fn = (
                jnp.where(highs[n], pltpu.roll(fp, d, 0), fp) + before * node,
                jnp.where(highs[n], fn, pltpu.roll(fn, SUBS - d, 0)) + after * node,
            )
            kept.append(r * node)
        rn, share, rp = factors[-1]
        first = (fp + share * fn) * rp
        last = rn * fn + share * first
        for n in reversed(range(len(levels))):
            r, before, after = factors[n + 1]
            node = kept[n + 1] + before * first + after * last
            first, last = jnp.where(highs[n], node, first), jnp.where(highs[n], last, node)
        r, before, after = factors[0]
        node = kept[0] + before * first + after * last
        solved.append(((first, node), (node, last)))
    for group in range(2):
        value = [solved[s][group][1] for s in range(species)]
        for i in reversed(range(half)):
            r, rk, ra = yr_ref[group, i], yk_ref[group, i], ya_ref[group, i]
            for s in range(species):
                value[s] = r * vt_ref[s, at_step(group, i), :] + ra * solved[s][group][0] + rk * value[s]
                vt_ref[s, at_step(group, i), :] = value[s]
    for s in range(species):
        for lo in range(0, ny, LANES):
            lanes = pl.ds(lo, LANES)
            pieces = [vt_ref[s, apart(lo + y, 2 * half), :] for y in range(0, LANES, SUBS)]
            m_ref[s, :, lanes] = c_ref[s, :, lanes] + 2.0 * jnp.concatenate(pieces, axis=0).T
    odd = lax.axis_index(axes[1]) & 1 == 1
    for part in range(0, nx, SUBS):
        here = pl.ds(part, SUBS)
        top, below_top = pl.ds(rows - nx + part, SUBS), pl.ds(rows - 2 * nx + part, SUBS)
        low, above_low = pl.ds(part, SUBS), pl.ds(nx + part, SUBS)
        m_top = [m_ref[s, top, :] for s in range(species)]
        m_low = [m_ref[s, low, :] for s in range(species)]
        k_top, k_low = kz_ref[below_top, :], kz_ref[low, :]
        for s in range(species):
            q_top = m_top[s] + reacted(table_ref, top, m_top, s) - k_top * (m_top[s] - m_ref[s, below_top, :])
            q_low = m_low[s] + reacted(table_ref, low, m_low, s) + k_low * (m_ref[s, above_low, :] - m_low[s])
            for n, (t, l) in enumerate(((m_top[s], m_low[s]), (q_top, q_low))):
                up_ref[n * species + s, here, :] = jnp.where(odd, l, t)
                down_ref[n * species + s, here, :] = jnp.where(odd, t, l)
        up_ref[2 * species, here, :] = jnp.where(odd, rz_ref[low, :], rz_ref[top, :])
        down_ref[2 * species, here, :] = jnp.where(odd, rz_ref[top, :], rz_ref[low, :])


def inner_passes(dims, m_ref, kz_ref, table_ref, p_ref, base_ref, out_hbm, sems):
    species, nz, nx, _, _ = dims

    def one_pass(source, target, z):
        for part in range(0, nx, SUBS):
            row = z * nx + part
            at = pl.ds(row, SUBS)
            amounts = [source[s, at, :] for s in range(species)]
            for s in range(species):
                total = amounts[s] + reacted(table_ref, at, amounts, s)
                if z < nz - 1:
                    total = total + kz_ref[at, :] * (source[s, pl.ds(row + nx, SUBS), :] - amounts[s])
                if z > 0:
                    total = total - kz_ref[pl.ds(row - nx, SUBS), :] * (amounts[s] - source[s, pl.ds(row - nx, SUBS), :])
                target[s, at, :] = total

    copies = []
    for z in range(nz + 1):
        if z < nz:
            one_pass(m_ref, p_ref, z)
        if z == 0:
            continue
        one_pass(p_ref, base_ref, z - 1)
        if 2 <= z - 1 < nz - 2:
            planes = pl.ds((z - 1) * nx, nx)
            copies.append(pltpu.make_async_copy(base_ref.at[:, planes, :], out_hbm.at[:, planes, :], sems.at[len(copies)]))
            copies[-1].start()
    for copy in copies:
        copy.wait()


def outer_side(dims, axis, planes, start, m_ref, p_ref, base_ref, got_ref, kz_ref, rz_ref, table_ref, part_hbm, out_hbm,
               edge_ref, next_ref, sems):
    species, nz, nx, _, _ = dims
    place = lax.axis_index(axis)
    top = (place + start) & 1 == 0
    exists = jnp.where(top, place < planes - 1, place > 0)
    rows_of = lambda up, low: pl.multiple_of(jnp.where(top, up * nx, low * nx), SUBS)
    edge_row, next_row, face_row = rows_of(nz - 1, 0), rows_of(nz - 2, 1), rows_of(nz - 2, 0)
    for part in range(0, nx, SUBS):
        here = pl.ds(part, SUBS)
        at, next_at = pl.ds(edge_row + part, SUBS), pl.ds(next_row + part, SUBS)
        k = jnp.where(exists, face(rz_ref[at, :], got_ref[2 * species, here, :]), 0.0)
        inside = kz_ref[pl.ds(face_row + part, SUBS), :]
        flux = [k * (got_ref[s, here, :] - m_ref[s, at, :]) for s in range(species)]
        for s in range(species):
            across = inside * flux[s]
            next_ref[s, here, :] = base_ref[s, next_at, :] + across
            difference = got_ref[species + s, here, :] - flux[s] - (p_ref[s, at, :] + flux[s])
            edge_ref[s, here, :] = (
                base_ref[s, at, :] + flux[s] - across + reacted(table_ref, at, flux, s) + k * difference
            )
    copies = [
        pltpu.make_async_copy(next_ref, out_hbm.at[:, pl.ds(next_row, nx), :], sems.at[0]),
        pltpu.make_async_copy(edge_ref, out_hbm.at[:, pl.ds(edge_row, nx), :], sems.at[1]),
    ]
    for copy in copies:
        copy.start()
    for copy in copies:
        copy.wait()


def involution(size, step):
    return [(i, i ^ step) for i in range(size)]


def halo_pairs(gx, gz, start):
    pairs = []
    for j in range(gz):
        partner = j + 1 if (j - start) % 2 == 0 else j - 1
        for i in range(gx):
            if 0 <= partner < gz:
                pairs.append((i * gz + j, i * gz + partner))
            else:
                pairs.append((i * gz + j, (i ^ 1) * gz + j))
    return pairs


def shards(concentration, facies, x_rates, y_rates, z_rates, react_table, gx, gz):
    species, nz, nx, ny = concentration.shape
    classes = x_rates.shape[0]
    dims = (species, nz, nx, ny, classes)
    axes = ("gx", "gz")
    rows = nz * nx
    half = ny // SUBS // 2
    f32 = jnp.float32
    shape = lambda *d: jax.ShapeDtypeStruct(d, f32)
    scratch = lambda *d: pltpu.VMEM(d, f32)
    dma = lambda n: pltpu.SemaphoreType.DMA((n,))

    def call(kernel, out_shape, in_specs, out_specs=None, scratch_shapes=(), **options):
        return pl.pallas_call(
            kernel,
            out_shape=out_shape,
            in_specs=in_specs,
            out_specs=out_specs or [VMEM] * len(out_shape),
            scratch_shapes=list(scratch_shapes),
            compiler_params=pltpu.CompilerParams(vmem_limit_bytes=8 << 20),
            **options,
        )

    in_hbm = lambda array: pltpu.with_memory_space_constraint(array, pltpu.HBM)
    react = jnp.transpose(react_table, (1, 2, 0))
    c = concentration.reshape(species, rows, ny)
    fac = facies.reshape(rows, ny)
    rounds = gx.bit_length() - 1
    assert gx == 1 << rounds and rounds > 2 and gz > 1 and nz > 4
    count, few = 3 + 2 * species, 1 + species
    blocks = ny // LANES

    ends, rk, ra, h, ry, c, fac = call(
        functools.partial(eliminate_x, dims),
        [shape(count, nz, ny), shape(nx, nz, ny), shape(nx, nz, ny), shape(species, nx, nz, ny), shape(rows, ny),
         shape(species, rows, ny), jax.ShapeDtypeStruct((rows, ny), jnp.int32)],
        [HBM] * 4,
        scratch_shapes=[scratch(species, blocks, rows + nz, LANES), scratch(blocks, rows + nz, LANES), scratch(rows, ny),
                        scratch(nx, nz, ny),
                        pltpu.SMEM((classes,), f32), pltpu.SMEM((classes,), f32), dma(3 + species)],
    )(in_hbm(x_rates), in_hbm(y_rates), in_hbm(c), in_hbm(fac))

    y_fac = call(
        functools.partial(y_factors, dims),
        [shape(2, half, SUBS, rows)] * 3 + [shape(3 * (2 + len(sub_levels())), SUBS, rows)],
        [VMEM],
        scratch_shapes=[scratch(ny + SUBS, rows)],
    )(ry)
    kz, rz, table = call(
        functools.partial(z_tables, dims),
        [shape(rows - nx, ny), shape(rows, ny), shape(species * species, rows, ny)],
        [HBM, HBM, VMEM, ANY],
        scratch_shapes=[pltpu.SMEM((classes,), f32), pltpu.SMEM(react.shape, f32), dma(2)],
    )(in_hbm(z_rates), in_hbm(react), fac, ends)

    saved, own = [], ends
    side_work = [y_fac[3], table]
    for bit in range(rounds - 1):
        got = lax.ppermute(own, "gx", involution(gx, 1 << bit))
        final = bit == rounds - 2
        out_shape = [shape(few if final else count, nz, ny), shape(2 + species, nz, ny)] + [shape(few, nz, ny)] * final
        merged = call(
            functools.partial(merge_x, species, bit, final, "gx"), out_shape, [VMEM, VMEM, ANY]
        )(own, got, side_work[min(bit, 1)])
        own = merged[0]
        saved.append(merged[1])
    outer = merged[2]
    got = lax.ppermute(own, "gx", involution(gx, 1 << (rounds - 1)))

    def solve(*refs):
        n = len(saved)
        solve_lines(dims, axes, list(range(rounds)), refs[0], refs[1], refs[2], refs[3 : 3 + n], *refs[3 + n :])

    operands = [own, got, outer] + saved + [rk, ra, h, c] + list(y_fac) + [kz, rz, table]
    m, to_a, to_b = call(
        solve,
        [shape(species, rows, ny), shape(2 * species + 1, nx, ny), shape(2 * species + 1, nx, ny)],
        [VMEM] * len(operands),
        scratch_shapes=[scratch(species, blocks, rows + nz, LANES), scratch(species, ny + SUBS, rows)],
    )(*operands)

    got_a = lax.ppermute(to_a, axes, halo_pairs(gx, gz, 0))
    got_b = lax.ppermute(to_b, axes, halo_pairs(gx, gz, 1))
    p, base, out = call(
        functools.partial(inner_passes, dims),
        [shape(species, rows, ny)] * 3,
        [VMEM] * 3,
        [VMEM, VMEM, HBM],
        scratch_shapes=[dma(nz - 4)],
    )(m, kz, table)
    for start, got in ((0, got_a), (1, got_b)):
        (out,) = call(
            functools.partial(outer_side, dims, "gz", gz, start),
            [shape(species, rows, ny)],
            [VMEM] * 7 + [HBM],
            [HBM],
            scratch_shapes=[scratch(species, nx, ny), scratch(species, nx, ny), dma(2)],
            input_output_aliases={7: 0},
        )(m, p, base, got, kz, rz, table, out)
    return out.reshape(concentration.shape)


def solution(mesh):
    in_specs = (P(None, "gz", "gx", None), P("gz", "gx", None), P(), P(), P(), P())
    out_specs = P(None, "gz", "gx", None)
    body = functools.partial(shards, gx=mesh.shape["gx"], gz=mesh.shape["gz"])
    return jax.shard_map(body, mesh=mesh, in_specs=in_specs, out_specs=out_specs, check_vma=False)
```

```python
import functools
import jax
import jax.numpy as jnp
from jax import lax
from jax.experimental import pallas as pl
from jax.experimental.pallas import tpu as pltpu
from jax.sharding import PartitionSpec as P

LANES = 128
SUBS = 8

VMEM = pl.BlockSpec(memory_space=pltpu.VMEM)
ANY = pl.BlockSpec(memory_space=pl.ANY)
HBM = pl.BlockSpec(memory_space=pltpu.HBM)


def face(a, b):
    return 2.0 * a * b / (a + b)


def picked(table, masks):
    value = table(0)
    for index, mask in masks:
        value = jnp.where(mask, table(index), value)
    return value


def class_masks(facies, classes):
    return [(index, facies == index) for index in range(1, classes)]


def merge_blocks(left, right):
    g1, lp, lq = left
    g2, lm, ln = right
    leak = lq + lm
    r = 1.0 / (g1 + g2 + leak)
    before, after = g1 * r, g2 * r
    return (g1 * after, lp + before * leak, ln + after * leak), (r, before, after)


def apart(row, length):
    return pl.ds(row + row // length, SUBS)


def spread(ref, at, value):
    for lo in range(0, value.shape[1], LANES):
        ref[lo // LANES, at, :] = value[:, lo : lo + LANES]


def eliminate_x(dims, xr_hbm, yr_hbm, c_hbm, fac_hbm, ends_ref, rk_ref, ra_ref, f_ref, r_ref, ry_ref, c_ref, fac_ref,
                e_ref, rx_ref, ky_ref, x_rates, y_rates, sems):
    species, nz, nx, ny, classes = dims
    rows = nz * nx
    copies = [
        pltpu.make_async_copy(fac_hbm, fac_ref, sems.at[0]),
        pltpu.make_async_copy(xr_hbm, x_rates, sems.at[1]),
        pltpu.make_async_copy(yr_hbm, y_rates, sems.at[2]),
    ]
    arrivals = [pltpu.make_async_copy(c_hbm.at[s], c_ref.at[s], sems.at[3 + s]) for s in range(species)]
    for copy in copies + arrivals:
        copy.start()
    lane = lax.broadcasted_iota(jnp.int32, (SUBS, ny), 1)
    not_last = lane < ny - 1
    for copy in copies:
        copy.wait()
    for row in range(0, rows, SUBS):
        at = pl.ds(row, SUBS)
        masks = class_masks(fac_ref[at, :], classes)
        spread(rx_ref, apart(row, nx), picked(lambda i: x_rates[i], masks))
        ry = picked(lambda i: y_rates[i], masks)
        ry_ref[at, :] = ry
        ky_ref[at, :] = jnp.where(not_last, face(ry, pltpu.roll(ry, ny - 1, 1)), 0.0)
    row_at = [pl.ds(x, nz, stride=nx + 1) for x in range(nx)]

    def explicit(s, row):
        at = pl.ds(row, SUBS)
        c = c_ref[s, at, :]
        flux = ky_ref[at, :] * (pltpu.roll(c, ny - 1, 1) - c)
        spread(e_ref.at[s], apart(row, nx), c + (flux - pltpu.roll(flux, 1, 1)))

    def coefficients(block):
        lanes = pl.ds(block * LANES, LANES)
        rate = rx_ref[block, row_at[0], :]
        a = 2.0 * rate
        excess = jnp.ones_like(a)
        leak = jnp.zeros_like(a)
        for x in range(nx):
            if x < nx - 1:
                rate_next = rx_ref[block, row_at[x + 1], :]
                k = face(rate, rate_next)
                rate = rate_next
            else:
                k = 2.0 * rate
            r = 1.0 / (a + excess + k)
            rk, ra = k * r, a * r
            r_ref[x, :, lanes] = r
            rk_ref[x, :, lanes] = rk
            ra_ref[x, :, lanes] = ra
            leak = leak + ra * excess
            a = a * rk
            excess = rk * excess
            if x < nx - 1:
                excess = 1.0 + excess
        for i, value in enumerate([a, leak, excess]):
            ends_ref[i, :, lanes] = value

    def sources(which, block):
        lanes = pl.ds(block * LANES, LANES)
        f = {s: e_ref[s, block, row_at[0], :] for s in which}
        first = {}
        for x in range(nx):
            rk, ra = rk_ref[x, :, lanes], ra_ref[x, :, lanes]
            for s in which:
                f_ref[s, x, :, lanes] = f[s]
                gain = ra * f[s]
                first[s] = gain if x == 0 else first[s] + gain
                f[s] = rk * f[s]
                if x < nx - 1:
                    f[s] = f[s] + e_ref[s, block, row_at[x + 1], :]
        for s in which:
            ends_ref[3 + s, :, lanes] = first[s]
            ends_ref[3 + species + s, :, lanes] = f[s]

    blocks = range(ny // LANES)
    for s in range(species):
        arrivals[s].wait()
        for row in range(0, rows, SUBS):
            explicit(s, row)
        for block in blocks:
            if s == 0:
                coefficients(block)
            elif s == species // 2:
                sources(range(s), block)
    for block in blocks:
        sources(range(species // 2, species), block)


def side_of(axis, bit):
    return (lax.axis_index(axis) >> bit) & 1 == 1


def emit_block(final, next_side, block, fp, fn, lanes, out_ref, outer_ref):
    species = len(fp)
    if not final:
        for i, value in enumerate(list(block) + list(fp) + list(fn)):
            out_ref[i, :, lanes] = value
        return
    pick = lambda a, b: jnp.where(next_side, a, b)
    g, leak_p, leak_n = block
    leak_out, leak_in = pick(leak_n, leak_p), pick(leak_p, leak_n)
    r = 1.0 / (g + leak_out)
    share = g * r
    out_ref[0, :, lanes] = leak_in + share * leak_out
    outer_ref[0, :, lanes] = share
    for s in range(species):
        f_out, f_in = pick(fn[s], fp[s]), pick(fp[s], fn[s])
        out_ref[1 + s, :, lanes] = f_in + share * f_out
        outer_ref[1 + s, :, lanes] = r * f_out


def merge_x(species, bit, final, axes, own_ref, got_ref, after_ref, out_ref, saved_ref, outer_ref=None, *rate_refs):
    side, next_side = side_of(axes[0], bit), side_of(axes[0], bit + 1)
    if final:
        odd = side_of(axes[1], 0)
        nx = rate_refs[0].shape[0]
        low, top = after_ref[pl.ds(0, nx), :], after_ref[pl.ds(after_ref.shape[0] - nx, nx), :]
        rate_refs[0][...] = jnp.where(odd, low, top)
        rate_refs[1][...] = jnp.where(odd, top, low)
    for lo in range(0, own_ref.shape[2], LANES):
        lanes = pl.ds(lo, LANES)
        own = [own_ref[i, :, lanes] for i in range(3 + 2 * species)]
        got = [got_ref[i, :, lanes] for i in range(3 + 2 * species)]
        left = [jnp.where(side, b, a) for a, b in zip(own, got)]
        right = [jnp.where(side, a, b) for a, b in zip(own, got)]
        block, (r, before, after) = merge_blocks(left[:3], right[:3])
        saved_ref[0, :, lanes] = before
        saved_ref[1, :, lanes] = after
        fp, fn = [], []
        for s in range(species):
            node = left[3 + species + s] + right[3 + s]
            fp.append(left[3 + s] + before * node)
            fn.append(right[3 + species + s] + after * node)
            saved_ref[2 + s, :, lanes] = r * node
        emit_block(final, next_side, block, fp, fn, lanes, out_ref, outer_ref)


def sub_levels():
    return [1 << n for n in range(SUBS.bit_length() - 1)]


def y_factors(dims, ry_ref, f_ref, r_ref, yr_ref, yk_ref, ya_ref, lv_ref, h_ref, rt_ref):
    species, nz, nx, ny, _ = dims
    for x in range(nx):
        r = r_ref[x]
        for s in range(species):
            h_ref[s, x] = r * f_ref[s, x]
    rows = nz * nx
    half = ny // SUBS // 2
    for lo in range(0, ny, LANES):
        turned = ry_ref[:, pl.ds(lo, LANES)].T
        for y in range(0, LANES, SUBS):
            rt_ref[apart(lo + y, 2 * half), :] = turned[y : y + SUBS]
    sub = lax.broadcasted_iota(jnp.int32, (SUBS, rows), 0)

    blocks = []
    for group in range(2):
        rates = [rt_ref[pl.ds(group * half + i, SUBS, stride=2 * half + 1), :] for i in range(half)]
        a = 2.0 * rates[0]
        excess = jnp.ones_like(a)
        leak = jnp.zeros_like(a)
        for i in range(half):
            k = face(rates[i], rates[i + 1]) if i < half - 1 else 2.0 * rates[i]
            r = 1.0 / (a + excess + k)
            rk, ra = k * r, a * r
            yr_ref[group, i] = r
            yk_ref[group, i] = rk
            ya_ref[group, i] = ra
            leak = leak + ra * excess
            a = a * rk
            excess = rk * excess
            if i < half - 1:
                excess = 1.0 + excess
        blocks.append((a, leak, excess))
    block, factors = merge_blocks(*blocks)
    kept = list(factors)
    for d in sub_levels():
        high = sub & d != 0
        from_low = [pltpu.roll(v, d, 0) for v in block]
        from_high = [pltpu.roll(v, SUBS - d, 0) for v in block]
        left = [jnp.where(high, b, a) for a, b in zip(block, from_low)]
        right = [jnp.where(high, a, b) for a, b in zip(block, from_high)]
        block, factors = merge_blocks(left, right)
        kept += list(factors)
    g, leak_p, leak_n = block
    rn = 1.0 / (g + leak_n)
    kept += [rn, g * rn, 1.0 / (leak_p + g * leak_n * rn)]
    for i, value in enumerate(kept):
        lv_ref[i] = value


def z_tables(dims, z_hbm, react_hbm, fac_ref, after_ref, kz_ref, rz_ref, table_ref, z_rates, react, sems):
    species, nz, nx, _, classes = dims
    rows = nz * nx
    copies = [pltpu.make_async_copy(z_hbm, z_rates, sems.at[0]), pltpu.make_async_copy(react_hbm, react, sems.at[1])]
    for copy in copies:
        copy.start()
    for copy in copies:
        copy.wait()
    for row in range(0, rows, SUBS):
        at = pl.ds(row, SUBS)
        masks = class_masks(fac_ref[at, :], classes)
        rz_ref[at, :] = picked(lambda i: z_rates[i], masks)
        for t in range(species):
            for s in range(species):
                table_ref[t * species + s, at, :] = picked(lambda i: react[t, s, i], masks)
    for row in range(0, rows - nx, SUBS):
        kz_ref[pl.ds(row, SUBS), :] = face(rz_ref[pl.ds(row, SUBS), :], rz_ref[pl.ds(row + nx, SUBS), :])


def reacted(table_ref, at, amounts, t):
    species = len(amounts)
    total = table_ref[t * species, at, :] * amounts[0]
    for s in range(1, species):
        total = total + table_ref[t * species + s, at, :] * amounts[s]
    return total


def solve_lines(dims, axes, bits, own_ref, got_ref, outer_ref, saved_refs, rk_ref, ra_ref, h_ref, c_ref,
                yr_ref, yk_ref, ya_ref, lv_ref, kz_ref, table_ref,
                m_ref, up_ref, down_ref, u_ref, vt_ref):
    species, nz, nx, ny, _ = dims
    rows = nz * nx
    half = ny // SUBS // 2
    index = lax.axis_index(axes[0])
    sides = [(index >> bit) & 1 == 1 for bit in bits]
    for lo in range(0, ny, LANES):
        lanes = pl.ds(lo, LANES)
        inv = 1.0 / (own_ref[0, :, lanes] + got_ref[0, :, lanes])
        outer_share = outer_ref[0, :, lanes]
        level = [(saved[0, :, lanes], saved[1, :, lanes]) for saved in saved_refs]
        for s in range(species):
            inner = (own_ref[1 + s, :, lanes] + got_ref[1 + s, :, lanes]) * inv
            outer = outer_ref[1 + s, :, lanes] + outer_share * inner
            first = jnp.where(sides[-1], inner, outer)
            last = jnp.where(sides[-1], outer, inner)
            for n in reversed(range(len(saved_refs))):
                before, after = level[n]
                node = saved_refs[n][2 + s, :, lanes] + before * first + after * last
                first, last = jnp.where(sides[n], node, first), jnp.where(sides[n], last, node)
            value = last
            for x in reversed(range(nx)):
                value = h_ref[s, x, :, lanes] + ra_ref[x, :, lanes] * first + rk_ref[x, :, lanes] * value
                u_ref[s, lo // LANES, pl.ds(x, nz, stride=nx + 1), :] = value
    for s in range(species):
        for lo in range(0, ny, LANES):
            lanes = pl.ds(lo, LANES)
            pieces = [
                u_ref[s, lo // LANES, apart(row, nx), :] - c_ref[s, pl.ds(row, SUBS), lanes]
                for row in range(0, rows, SUBS)
            ]
            turned = jnp.concatenate(pieces, axis=0).T
            for y in range(0, LANES, SUBS):
                vt_ref[s, apart(lo + y, 2 * half), :] = turned[y : y + SUBS]

    def at_step(group, i):
        return pl.ds(group * half + i, SUBS, stride=2 * half + 1)

    sub = lax.broadcasted_iota(jnp.int32, (SUBS, rows), 0)
    ends = []
    for group in range(2):
        f = [vt_ref[s, at_step(group, 0), :] for s in range(species)]
        first = [None] * species
        for i in range(half):
            rk, ra = yk_ref[group, i], ya_ref[group, i]
            for s in range(species):
                gain = ra * f[s]
                first[s] = gain if i == 0 else first[s] + gain
                if i > 0:
                    vt_ref[s, at_step(group, i), :] = f[s]
                f[s] = rk * f[s]
                if i < half - 1:
                    f[s] = f[s] + vt_ref[s, at_step(group, i + 1), :]
        ends.append((first, f))
    levels = sub_levels()
    highs = [sub & d != 0 for d in levels]
    factors = [[lv_ref[3 * n + i] for i in range(3)] for n in range(len(levels) + 2)]
    solved = []
    for s in range(species):
        r, before, after = factors[0]
        node = ends[0][1][s] + ends[1][0][s]
        fp, fn = ends[0][0][s] + before * node, ends[1][1][s] + after * node
        kept = [r * node]
        for n, d in enumerate(levels):
            r, before, after = factors[n + 1]
            node = jnp.where(highs[n], fp + pltpu.roll(fn, d, 0), fn + pltpu.roll(fp, SUBS - d, 0))
            fp, fn = (
                jnp.where(highs[n], pltpu.roll(fp, d, 0), fp) + before * node,
                jnp.where(highs[n], fn, pltpu.roll(fn, SUBS - d, 0)) + after * node,
            )
            kept.append(r * node)
        rn, share, rp = factors[-1]
        first = (fp + share * fn) * rp
        last = rn * fn + share * first
        for n in reversed(range(len(levels))):
            r, before, after = factors[n + 1]
            node = kept[n + 1] + before * first + after * last
            first, last = jnp.where(highs[n], node, first), jnp.where(highs[n], last, node)
        r, before, after = factors[0]
        node = kept[0] + before * first + after * last
        solved.append(((first, node), (node, last)))
    for group in range(2):
        value = [solved[s][group][1] for s in range(species)]
        for i in reversed(range(half)):
            r, rk, ra = yr_ref[group, i], yk_ref[group, i], ya_ref[group, i]
            for s in range(species):
                value[s] = r * vt_ref[s, at_step(group, i), :] + ra * solved[s][group][0] + rk * value[s]
                vt_ref[s, at_step(group, i), :] = value[s]
    for s in range(species):
        for lo in range(0, ny, LANES):
            lanes = pl.ds(lo, LANES)
            pieces = [vt_ref[s, apart(lo + y, 2 * half), :] for y in range(0, LANES, SUBS)]
            m_ref[s, :, lanes] = c_ref[s, :, lanes] + 2.0 * jnp.concatenate(pieces, axis=0).T
    odd = lax.axis_index(axes[1]) & 1 == 1
    for part in range(0, nx, SUBS):
        here = pl.ds(part, SUBS)
        top, below_top = pl.ds(rows - nx + part, SUBS), pl.ds(rows - 2 * nx + part, SUBS)
        low, above_low = pl.ds(part, SUBS), pl.ds(nx + part, SUBS)
        m_top = [m_ref[s, top, :] for s in range(species)]
        m_low = [m_ref[s, low, :] for s in range(species)]
        k_top, k_low = kz_ref[below_top, :], kz_ref[low, :]
        for s in range(species):
            q_top = m_top[s] + reacted(table_ref, top, m_top, s) - k_top * (m_top[s] - m_ref[s, below_top, :])
            q_low = m_low[s] + reacted(table_ref, low, m_low, s) + k_low * (m_ref[s, above_low, :] - m_low[s])
            for n, (t, l) in enumerate(((m_top[s], m_low[s]), (q_top, q_low))):
                up_ref[n * species + s, here, :] = jnp.where(odd, l, t)
                down_ref[n * species + s, here, :] = jnp.where(odd, t, l)


def inner_passes(dims, m_ref, kz_ref, table_ref, p_ref, base_ref, out_hbm, sems):
    species, nz, nx, _, _ = dims

    def one_pass(source, target, z):
        for part in range(0, nx, SUBS):
            row = z * nx + part
            at = pl.ds(row, SUBS)
            amounts = [source[s, at, :] for s in range(species)]
            for s in range(species):
                total = amounts[s] + reacted(table_ref, at, amounts, s)
                if z < nz - 1:
                    total = total + kz_ref[at, :] * (source[s, pl.ds(row + nx, SUBS), :] - amounts[s])
                if z > 0:
                    total = total - kz_ref[pl.ds(row - nx, SUBS), :] * (amounts[s] - source[s, pl.ds(row - nx, SUBS), :])
                target[s, at, :] = total

    copies = []
    for z in range(nz + 1):
        if z < nz:
            one_pass(m_ref, p_ref, z)
        if z == 0:
            continue
        one_pass(p_ref, base_ref, z - 1)
        if 2 <= z - 1 < nz - 2:
            planes = pl.ds((z - 1) * nx, nx)
            copies.append(pltpu.make_async_copy(base_ref.at[:, planes, :], out_hbm.at[:, planes, :], sems.at[len(copies)]))
            copies[-1].start()
    for copy in copies:
        copy.wait()


def outer_side(dims, axis, planes, start, m_ref, p_ref, base_ref, got_ref, rate_ref, kz_ref, rz_ref, table_ref, part_hbm, out_hbm,
               edge_ref, next_ref, sems):
    species, nz, nx, _, _ = dims
    place = lax.axis_index(axis)
    top = (place + start) & 1 == 0
    exists = jnp.where(top, place < planes - 1, place > 0)
    rows_of = lambda up, low: pl.multiple_of(jnp.where(top, up * nx, low * nx), SUBS)
    edge_row, next_row, face_row = rows_of(nz - 1, 0), rows_of(nz - 2, 1), rows_of(nz - 2, 0)
    for part in range(0, nx, SUBS):
        here = pl.ds(part, SUBS)
        at, next_at = pl.ds(edge_row + part, SUBS), pl.ds(next_row + part, SUBS)
        k = jnp.where(exists, face(rz_ref[at, :], rate_ref[here, :]), 0.0)
        inside = kz_ref[pl.ds(face_row + part, SUBS), :]
        flux = [k * (got_ref[s, here, :] - m_ref[s, at, :]) for s in range(species)]
        for s in range(species):
            across = inside * flux[s]
            next_ref[s, here, :] = base_ref[s, next_at, :] + across
            difference = got_ref[species + s, here, :] - flux[s] - (p_ref[s, at, :] + flux[s])
            edge_ref[s, here, :] = (
                base_ref[s, at, :] + flux[s] - across + reacted(table_ref, at, flux, s) + k * difference
            )
    copies = [
        pltpu.make_async_copy(next_ref, out_hbm.at[:, pl.ds(next_row, nx), :], sems.at[0]),
        pltpu.make_async_copy(edge_ref, out_hbm.at[:, pl.ds(edge_row, nx), :], sems.at[1]),
    ]
    for copy in copies:
        copy.start()
    for copy in copies:
        copy.wait()


def involution(size, step):
    return [(i, i ^ step) for i in range(size)]


def halo_pairs(gx, gz, start):
    pairs = []
    for j in range(gz):
        partner = j + 1 if (j - start) % 2 == 0 else j - 1
        for i in range(gx):
            if 0 <= partner < gz:
                pairs.append((i * gz + j, i * gz + partner))
            else:
                pairs.append((i * gz + j, (i ^ 1) * gz + j))
    return pairs


def shards(concentration, facies, x_rates, y_rates, z_rates, react_table, gx, gz):
    species, nz, nx, ny = concentration.shape
    classes = x_rates.shape[0]
    dims = (species, nz, nx, ny, classes)
    axes = ("gx", "gz")
    rows = nz * nx
    half = ny // SUBS // 2
    f32 = jnp.float32
    shape = lambda *d: jax.ShapeDtypeStruct(d, f32)
    scratch = lambda *d: pltpu.VMEM(d, f32)
    dma = lambda n: pltpu.SemaphoreType.DMA((n,))

    def call(kernel, out_shape, in_specs, out_specs=None, scratch_shapes=(), **options):
        return pl.pallas_call(
            kernel,
            out_shape=out_shape,
            in_specs=in_specs,
            out_specs=out_specs or [VMEM] * len(out_shape),
            scratch_shapes=list(scratch_shapes),
            compiler_params=pltpu.CompilerParams(vmem_limit_bytes=8 << 20),
            **options,
        )

    in_hbm = lambda array: pltpu.with_memory_space_constraint(array, pltpu.HBM)
    react = jnp.transpose(react_table, (1, 2, 0))
    c = concentration.reshape(species, rows, ny)
    fac = facies.reshape(rows, ny)
    rounds = gx.bit_length() - 1
    assert gx == 1 << rounds and rounds > 2 and gz > 1 and nz > 4
    count, few = 3 + 2 * species, 1 + species
    blocks = ny // LANES

    ends, rk, ra, f, r, ry, c, fac = call(
        functools.partial(eliminate_x, dims),
        [shape(count, nz, ny), shape(nx, nz, ny), shape(nx, nz, ny), shape(species, nx, nz, ny), shape(nx, nz, ny), shape(rows, ny),
         shape(species, rows, ny), jax.ShapeDtypeStruct((rows, ny), jnp.int32)],
        [HBM] * 4,
        scratch_shapes=[scratch(species, blocks, rows + nz, LANES), scratch(blocks, rows + nz, LANES), scratch(rows, ny),
                        pltpu.SMEM((classes,), f32), pltpu.SMEM((classes,), f32), dma(3 + species)],
    )(in_hbm(x_rates), in_hbm(y_rates), in_hbm(c), in_hbm(fac))

    *y_fac, h = call(
        functools.partial(y_factors, dims),
        [shape(2, half, SUBS, rows)] * 3 + [shape(3 * (2 + len(sub_levels())), SUBS, rows), shape(species, nx, nz, ny)],
        [VMEM] * 3,
        scratch_shapes=[scratch(ny + SUBS, rows)],
    )(ry, f, r)
    kz, rz, table = call(
        functools.partial(z_tables, dims),
        [shape(rows - nx, ny), shape(rows, ny), shape(species * species, rows, ny)],
        [HBM, HBM, VMEM, ANY],
        scratch_shapes=[pltpu.SMEM((classes,), f32), pltpu.SMEM(react.shape, f32), dma(2)],
    )(in_hbm(z_rates), in_hbm(react), fac, ends)

    saved, own = [], ends
    for bit in range(rounds - 1):
        got = lax.ppermute(own, "gx", involution(gx, 1 << bit))
        final = bit == rounds - 2
        out_shape = [shape(few if final else count, nz, ny), shape(2 + species, nz, ny)]
        out_shape += [shape(few, nz, ny), shape(nx, ny), shape(nx, ny)] * final
        merged = call(
            functools.partial(merge_x, species, bit, final, axes), out_shape, [VMEM, VMEM, VMEM if final else ANY]
        )(own, got, rz if final else y_fac[3] if bit == 0 else table)
        own = merged[0]
        saved.append(merged[1])
    outer, rate_a, rate_b = merged[2:]
    got = lax.ppermute(own, "gx", involution(gx, 1 << (rounds - 1)))

    rate_a = lax.ppermute(rate_a, axes, halo_pairs(gx, gz, 0))
    rate_b = lax.ppermute(rate_b, axes, halo_pairs(gx, gz, 1))

    def solve(*refs):
        n = len(saved)
        solve_lines(dims, axes, list(range(rounds)), refs[0], refs[1], refs[2], refs[3 : 3 + n], *refs[3 + n :])

    operands = [own, got, outer] + saved + [rk, ra, h, c] + list(y_fac) + [kz, table]
    m, to_a, to_b = call(
        solve,
        [shape(species, rows, ny), shape(2 * species, nx, ny), shape(2 * species, nx, ny)],
        [VMEM] * len(operands),
        scratch_shapes=[scratch(species, blocks, rows + nz, LANES), scratch(species, ny + SUBS, rows)],
    )(*operands)

    got_a = lax.ppermute(to_a, axes, halo_pairs(gx, gz, 0))
    got_b = lax.ppermute(to_b, axes, halo_pairs(gx, gz, 1))
    p, base, out = call(
        functools.partial(inner_passes, dims),
        [shape(species, rows, ny)] * 3,
        [VMEM] * 3,
        [VMEM, VMEM, HBM],
        scratch_shapes=[dma(nz - 4)],
    )(m, kz, table)
    for start, got, rate in ((0, got_a, rate_a), (1, got_b, rate_b)):
        (out,) = call(
            functools.partial(outer_side, dims, "gz", gz, start),
            [shape(species, rows, ny)],
            [VMEM] * 8 + [HBM],
            [HBM],
            scratch_shapes=[scratch(species, nx, ny), scratch(species, nx, ny), dma(2)],
            input_output_aliases={8: 0},
        )(m, p, base, got, rate, kz, rz, table, out)
    return out.reshape(concentration.shape)


def solution(mesh):
    in_specs = (P(None, "gz", "gx", None), P("gz", "gx", None), P(), P(), P(), P())
    out_specs = P(None, "gz", "gx", None)
    body = functools.partial(shards, gx=mesh.shape["gx"], gz=mesh.shape["gz"])
    return jax.shard_map(body, mesh=mesh, in_specs=in_specs, out_specs=out_specs, check_vma=False)
```
